512 devices in a mesh: section: 8 (over y, x_hi), ctx: 16 (over z), dp: 4 (over x_lo, core).
Axes of the slice: x: 4 (x_hi: 2, x_lo: 2; x = x_hi * 2 + x_lo), y: 4, z: 16, core: 2. Of those that a mesh axis runs over, the one named last changes fastest.
Arguments:
- activations: bfloat16 [8, 4, 2048, 1280], P('section', 'dp', 'ctx'), may hold values from -6 to 6
- out_grads: bfloat16 [8, 4, 2048, 1280], P('section', 'dp', 'ctx'), may hold values from -6 to 6
- doc_ids: int32 [4, 16], replicated, may hold values from 0 to 3, never falling along the last dimension, each value on 1 to 12 neighbouring positions
- query_weight: bfloat16 [8, 1280, 640], P('section', None, 'dp'), may hold values from -0.195655948 to 0.195655948
- key_weight: bfloat16 [8, 1280, 640], P('section', None, 'dp'), may hold values from -3.0745935 to 3.0745935
- value_weight: bfloat16 [8, 1280, 640], P('section', None, 'dp'), may hold values from -0.15625 to 0.15625
- out_weight: bfloat16 [8, 640, 1280], P('section', 'dp'), may hold values from -0.25 to 0.25
Outputs:
- received_grad: bfloat16 [8, 4, 2048, 1280], P('section', 'dp', 'ctx')
The draws below stay inside these ranges and needn't reach their ends.
Inputs may be any that keep to these rules, and one draw needn't show every extreme that they name: `doc_ids`: each page stack's documents are runs of whole blocks, numbered from 0 in order; a document covers at most 12 blocks.
All inputs are finite; a program needn't handle non-finite values.
Results may differ from the reference program's by a relative error of at most 0.0085.
The reference program's roundings to bfloat16 on the way count: a program that leaves them out, or rounds other values in their place, can miss the bound.
Values may be sent and summed in bfloat16 or wider, within the bound.
A program may use at most 128 MiB of HBM per device.

```python
import math
import jax
import jax.numpy as jnp
import numpy as np
from jax import lax

D = 1280
HEADS = 8
HEAD_DIM = 80
BLOCK = 128
LENGTH = 2048
NB = 16
PAGES = 4
N_SECTION = 8


def weight_base(key):
    raw = jax.random.normal(jax.random.fold_in(key, 11), (N_SECTION, D, HEADS * HEAD_DIM), jnp.float32)
    return jnp.clip(raw, -4.0, 4.0) * (1.7 * D ** (-0.5))


def draw_query_weight(key, part):
    return weight_base(key).astype(jnp.bfloat16)


def draw_key_weight(key, part):
    raw = jax.random.normal(jax.random.fold_in(key, 12), (N_SECTION, D, HEADS * HEAD_DIM), jnp.float32)
    result = jnp.clip(raw, -4.0, 4.0) * D ** (-0.5)
    return result.astype(jnp.bfloat16)


def draw_activations(key, part):
    shape = (N_SECTION, PAGES, LENGTH, D)
    result = jnp.clip(jax.random.normal(jax.random.fold_in(key, 23), shape, jnp.float32), -6.0, 6.0)
    return result.astype(jnp.bfloat16)


def steps_of(key, dims, cuts, least, high):
    loudness = 1.0
    for dim, blocks in cuts:
        steps = jax.random.uniform(jax.random.fold_in(jax.random.fold_in(key, 6), dim), (blocks,), jnp.float32, least / len(cuts), high / len(cuts))
        loudness = loudness * jnp.repeat(jnp.exp(steps), dims[dim] // blocks).reshape((-1,) + (1,) * (len(dims) - 1 - dim))
    return loudness


def length_profile(amount, total, reach, lean):
    portions = [(1 << 20) // math.isqrt(standing ** lean) + 1 for standing in range(2, amount + 1)]
    rest, holding = total - reach - (amount - 1), [1] * (amount - 1)
    while rest > 0:
        movable = [i for i in range(amount - 1) if holding[i] < reach]
        mass, budget = sum([portions[i] for i in movable]), rest
        for i in movable:
            addition = min(reach - holding[i], max(1, budget * portions[i] // mass), rest)
            holding[i] = holding[i] + addition
            rest = rest - addition
    return np.array([reach] + holding)


def uneven_parts(rng, count, total, bound, slope):
    if count == 2:
        one = jax.random.randint(rng, (), max(1, total - bound), min(bound, total - 1) + 1)
        return jnp.stack([one, total - one])
    lengths = jnp.asarray(length_profile(count, total, bound, slope), jnp.int32)
    couples = (count - 1) // 2
    source_of, receiver = lengths[1:1 + 2 * couples:2], lengths[2:2 + 2 * couples:2]
    margin = jnp.minimum(source_of - 1, bound - receiver)
    shifted = jax.random.randint(jax.random.fold_in(rng, 1), (couples,), 0, 1 << 20) % (margin + 1)
    lengths = lengths.at[1:1 + 2 * couples:2].set(source_of - shifted).at[2:2 + 2 * couples:2].set(receiver + shifted)
    return lengths[jax.random.permutation(jax.random.fold_in(rng, 2), count)]


def scatter_about(rng, shape, spread, reach, shards=(), dtype=jnp.bfloat16):
    drawn = spread * jax.random.normal(rng, shape, jnp.float32)
    if shards:
        drawn = drawn * steps_of(rng, shape, shards, -0.22, 0.18)
    return jnp.clip(drawn, -reach, reach).astype(dtype)


def setup_inputs(seed: int = 0) -> dict:
    seeds = jax.random.split(jax.random.key(seed), 8)
    return {
        "activations": draw_activations(jax.random.fold_in(seeds[7], 71), 0),
        "out_grads": scatter_about(seeds[1], (N_SECTION, PAGES, LENGTH, D), 1.0, 6.0, ((0, 8), (1, 4), (2, 16))),
        "doc_ids": jax.vmap(lambda own: jnp.searchsorted(jnp.cumsum(uneven_parts(own, max(2, NB // 4), NB, 3 * NB // 4, 2)), jnp.arange(NB), side="right"))(jax.random.split(seeds[2], PAGES)).reshape((PAGES, NB)).astype(jnp.int32),
        "query_weight": draw_query_weight(jax.random.fold_in(seeds[7], 71), 0),
        "key_weight": draw_key_weight(jax.random.fold_in(seeds[7], 71), 0),
        "value_weight": scatter_about(seeds[5], (N_SECTION, D, HEADS * HEAD_DIM), D ** -0.5, 0.15625, ((0, 8), (2, 4))),
        "out_weight": scatter_about(seeds[6], (N_SECTION, HEADS * HEAD_DIM, D), (HEADS * HEAD_DIM) ** -0.5, 0.25, ((0, 8), (1, 4))),
    }


NEG = -1e+30

def layer_grad(inputs_low, upstream, page_ids, query_proj, key_proj, value_proj, out_proj):
    length = inputs_low.shape[0]
    score_scale = HEAD_DIM ** (-0.5)
    highest = lax.Precision.HIGHEST
    inputs = inputs_low.astype(jnp.float32)
    inv_rms = lax.rsqrt(lax.optimization_barrier(jnp.mean(inputs * inputs, axis=-1, keepdims=True)) + 1e-05)
    normed = (inputs * inv_rms).astype(jnp.bfloat16)
    queries = jnp.dot(normed, query_proj, preferred_element_type=jnp.float32)
    key_rows = jnp.dot(normed, key_proj, preferred_element_type=jnp.float32)
    values = jnp.dot(normed, value_proj, preferred_element_type=jnp.float32).astype(jnp.bfloat16)
    out_grad = jnp.dot(upstream, out_proj.T, preferred_element_type=jnp.float32).astype(jnp.bfloat16)
    block_doc = page_ids[(jnp.arange(length) // BLOCK).astype(jnp.int32)]
    allowed = block_doc[:, None] == block_doc[None, :]

    def split_heads(matrix):
        return matrix.reshape(length, HEADS, HEAD_DIM).transpose(1, 0, 2)

    def one_head(parts):
        head_q = parts[0].astype(jnp.float32)
        head_k = parts[1].astype(jnp.float32)
        head_v = parts[2].astype(jnp.float32)
        head_g = parts[3].astype(jnp.float32)
        scores = jnp.dot(head_q, head_k.T, precision=highest) * score_scale
        scores = jnp.where(allowed, scores, NEG)
        top_score = lax.optimization_barrier(jnp.max(scores, axis=-1, keepdims=True))
        total = lax.optimization_barrier(jnp.sum(jnp.where(allowed, jnp.exp(scores - top_score), 0.0), axis=-1, keepdims=True))
        log_total = top_score + jnp.log(total)
        prob = jnp.where(allowed, jnp.exp(scores - log_total), 0.0)
        dprob = jnp.dot(head_g, head_v.T, precision=highest)
        row_delta = lax.optimization_barrier(jnp.sum(prob * dprob, axis=-1, keepdims=True))
        dscore = prob * (dprob - row_delta)
        dscore_low = lax.optimization_barrier(dscore.astype(jnp.bfloat16)).astype(jnp.float32)
        prob_low = lax.optimization_barrier(prob.astype(jnp.bfloat16)).astype(jnp.float32)
        q_grad = (jnp.dot(dscore_low, head_k, precision=highest) * score_scale).astype(jnp.bfloat16)
        k_grad = (jnp.dot(dscore_low.T, head_q, precision=highest) * score_scale).astype(jnp.bfloat16)
        v_grad = jnp.dot(prob_low.T, head_g, precision=highest).astype(jnp.bfloat16)
        return (q_grad, k_grad, v_grad)
    head_grads = lax.map(one_head, (split_heads(queries), split_heads(key_rows), split_heads(values), split_heads(out_grad)))

    def merge_heads(stacked):
        return stacked.transpose(1, 0, 2).reshape(length, HEADS * HEAD_DIM)
    q_grad = merge_heads(head_grads[0])
    k_grad = merge_heads(head_grads[1])
    v_grad = merge_heads(head_grads[2])
    normed_grad = jnp.dot(q_grad, query_proj.T, preferred_element_type=jnp.float32)
    normed_grad = normed_grad + jnp.dot(k_grad, key_proj.T, preferred_element_type=jnp.float32)
    normed_grad = normed_grad + jnp.dot(v_grad, value_proj.T, preferred_element_type=jnp.float32)
    branch = inv_rms * normed_grad - inputs * inv_rms ** 3 * lax.optimization_barrier(jnp.mean(normed_grad * inputs, axis=-1, keepdims=True))
    return branch.astype(jnp.bfloat16)

def reference(activations, out_grads, doc_ids, query_weight, key_weight, value_weight, out_weight):

    def per_section(section_parts):
        section_inputs, section_upstream, section_q, section_k, section_v, section_o = section_parts

        def per_page(page_parts):
            return layer_grad(page_parts[0], page_parts[1], page_parts[2], section_q, section_k, section_v, section_o)
        return lax.map(per_page, (section_inputs, section_upstream, doc_ids))
    branches = lax.map(per_section, (activations, out_grads, query_weight, key_weight, value_weight, out_weight))
    return jnp.roll(branches, -1, axis=0)
```

```python
import functools

import jax
import jax.numpy as jnp
from jax import lax
from jax.experimental import pallas as pl
from jax.experimental.pallas import tpu as pltpu
from jax.sharding import PartitionSpec as P

HEAD_DIM = 80
BLOCK = 128
WIDTH = 1280
N_CTX = 16
HALF = 8
SCALE = HEAD_DIM ** (-0.5)
NEG = -1e30
H1, H2, H3, H4, H6 = (n * HEAD_DIM for n in (1, 2, 3, 4, 6))
F32 = jnp.float32
BF16 = jnp.bfloat16
NT = (((1,), (1,)), ((), ()))


def dot(a, b):
    return jnp.dot(a, b, preferred_element_type=F32)


def dot_nt(a, b):
    return lax.dot_general(a, b, NT, preferred_element_type=F32)


def flip(matrix):
    return matrix.astype(F32).T.astype(BF16)


def split(wide):
    high = wide.astype(BF16)
    return high, (wide - high.astype(F32)).astype(BF16)


def kernel(
    docs_ref,
    doc_row_ref,
    x_ref,
    og_ref,
    w_ref,
    out_ref,
    weights,
    normed,
    send,
    recv,
    kv_other,
    keys3,
    values,
    kv_grad,
    kv_partial,
    back_q,
    back_kv,
    got_q,
    got_kv,
    total,
    branch_out,
    w_send,
    relay_send,
    w_recv,
    send_sem,
    recv_sem,
    kv_send,
    kv_recv,
    part_send,
    part_recv,
    bq_send,
    bq_recv,
    bkv_send,
    bkv_recv,
    out_send,
    out_recv,
):
    section = lax.axis_index("section")
    n_section = lax.axis_size("section")
    z = lax.axis_index("ctx")
    dp = lax.axis_index("dp")
    x, c = dp // 2, dp % 2
    z_half, z_low = z // HALF, z % HALF
    core_peer = {"dp": 2 * x + 1 - c}
    x_peer = {"dp": 2 * (1 - x) + c}
    before = {"section": (section + n_section - 1) % n_section}
    after = {"section": (section + 1) % n_section}
    alone = z_half == c

    def peer(index):
        return {"ctx": HALF * c + index, "dp": 2 * x + z_half}

    barrier = pltpu.get_barrier_semaphore()
    for other in (core_peer, x_peer, before, after):
        pl.semaphore_signal(barrier, inc=1, device_id=other)

    def greet(index, carry):
        @pl.when(jnp.logical_not(alone & (index == z_low)))
        def _():
            pl.semaphore_signal(barrier, inc=1, device_id=peer(index))

        return carry

    lax.fori_loop(0, HALF, greet, 0)

    def weight_slot(r, j):
        return 4 * j + 2 * ((x + r // 2) % 2) + (c + r % 2) % 2

    def own_weights(j):
        return pltpu.make_async_copy(w_ref.at[j], weights.at[weight_slot(0, j)], w_recv.at[0, j])

    def pass_weights(r, j, target, send_sem_ref, arrive_r):
        block = weights.at[weight_slot(r, j)]
        return pltpu.make_async_remote_copy(
            src_ref=block,
            dst_ref=block,
            send_sem=send_sem_ref,
            recv_sem=w_recv.at[arrive_r, j],
            device_id=target,
        )

    def to_x(j):
        return pass_weights(0, j, x_peer, w_send.at[0, j], 2)

    def to_core(j):
        return pass_weights(0, j, core_peer, w_send.at[1, j], 1)

    def relay(j):
        return pass_weights(2, j, core_peer, relay_send.at[j], 3)

    def weights_here(r, j):
        block = weights.at[weight_slot(r, j)]
        pltpu.make_async_copy(block, block, w_recv.at[r, j]).wait()

    for j in range(2):
        own_weights(j).start()

    inputs = x_ref[...].astype(F32)
    inv_rms = lax.rsqrt(jnp.mean(inputs * inputs, axis=-1, keepdims=True) + 1e-05)
    normed[...] = (inputs * inv_rms).astype(BF16)

    own_weights(0).wait()
    own_weights(1).wait()
    pl.semaphore_wait(barrier, 12 - alone.astype(jnp.int32))
    for j in range(2):
        to_x(j).start()
    for j in range(2):
        to_core(j).start()

    def send_copy(index):
        return pltpu.make_async_remote_copy(
            src_ref=send.at[index],
            dst_ref=recv.at[z_low],
            send_sem=send_sem.at[index],
            recv_sem=recv_sem.at[z_low],
            device_id=peer(index),
        )

    def project(slot):
        w = weights.at[slot]
        qkv = dot_nt(w[0:H3], normed[...])
        out_grad = dot_nt(w[H3:H4], og_ref[...])
        q_high, q_low = split(qkv[0:H1])
        k_high, k_low = split(qkv[H1:H2])
        message = send.at[slot]
        message[0:H1] = q_high
        message[H1:H2] = q_low
        message[H2:H3] = out_grad.astype(BF16)
        message[H3:H4] = k_high
        message[H4 : H4 + H1] = k_low
        message[H4 + H1 : H6] = qkv[H2:H3].astype(BF16)
        mine = alone & (slot == z_low)

        @pl.when(mine)
        def _():
            pltpu.make_async_copy(message, recv.at[z_low], recv_sem.at[z_low]).start()

        @pl.when(jnp.logical_not(mine))
        def _():
            send_copy(slot).start()

    def near(t, carry):
        r, j = t // 2, t % 2

        @pl.when(r == 1)
        def _():
            weights_here(1, j)

        project(weight_slot(r, j))
        return carry

    lax.fori_loop(0, 4, near, 0)

    def far(t, carry):
        r, j = 2 + t % 2, t // 2
        weights_here(r, j)

        @pl.when(r == 2)
        def _():
            relay(j).start()

        project(weight_slot(r, j))
        return carry

    lax.fori_loop(0, 4, far, 0)

    def kv_copy(index):
        return pltpu.make_async_remote_copy(
            src_ref=recv.at[index, pl.ds(H3, H3)],
            dst_ref=kv_other.at[index],
            send_sem=kv_send.at[index],
            recv_sem=kv_recv.at[index],
            device_id=core_peer,
        )

    def place(block, kv):
        lanes = pl.ds(pl.multiple_of(block * BLOCK, BLOCK), BLOCK)
        keys3[0:H2, lanes] = kv[0:H2]
        keys3[H2:H3, lanes] = kv[0:H1]
        values[:, lanes] = kv[H2:H3]

    def arrive(index, carry):
        block = recv.at[index]
        pltpu.make_async_copy(block, block, recv_sem.at[index]).wait()
        kv_copy(index).start()
        place(HALF * c + index, recv[index, H3:H6])
        return carry

    lax.fori_loop(0, HALF, arrive, 0)

    def arrive_other(index, carry):
        kv_copy(index).wait_recv()
        place(HALF * (1 - c) + index, kv_other[index])
        return carry

    lax.fori_loop(0, HALF, arrive_other, 0)

    page = 2 * x + z_half
    doc_row = doc_row_ref[page]
    kv_grad[...] = jnp.zeros_like(kv_grad)

    def return_q(index):
        return pltpu.make_async_remote_copy(
            src_ref=back_q.at[index],
            dst_ref=got_q.at[z_low],
            send_sem=bq_send.at[index],
            recv_sem=bq_recv.at[z_low],
            device_id=peer_back(index),
        )

    def return_kv(index):
        return pltpu.make_async_remote_copy(
            src_ref=back_kv.at[index],
            dst_ref=got_kv.at[z_low],
            send_sem=bkv_send.at[index],
            recv_sem=bkv_recv.at[z_low],
            device_id=peer_back(index),
        )

    def peer_back(index):
        return peer(index)

    def attend(chunk, carry):
        one, two = recv.at[2 * chunk], recv.at[2 * chunk + 1]
        q_pair = jnp.concatenate([one[0:H2], two[0:H2]], axis=1)
        g_flat = jnp.concatenate([one[H2:H3], two[H2:H3]], axis=1)
        q3 = flip(jnp.concatenate([q_pair[0:H1], q_pair], axis=0))
        g = flip(g_flat)
        first = docs_ref[page, HALF * c + 2 * chunk]
        second = docs_ref[page, HALF * c + 2 * chunk + 1]
        rows = lax.broadcasted_iota(jnp.int32, (2 * BLOCK, 1), 0)
        allowed = jnp.where(rows < BLOCK, first, second) == doc_row
        scores = jnp.where(allowed, dot(q3, keys3[...]) * SCALE, NEG)
        top = jnp.max(scores, axis=-1, keepdims=True)
        weight = jnp.exp(scores - top)
        share = 1.0 / jnp.sum(weight, axis=-1, keepdims=True)
        prob = weight * share
        dprob = dot(g, values[...])
        delta = jnp.sum(prob * dprob, axis=-1, keepdims=True)
        dscore = (prob * (dprob - delta)).astype(BF16)
        q_grad = dot_nt(keys3[0:H2], dscore)
        q_grad = ((q_grad[0:H1] + q_grad[H1:H2]) * SCALE).astype(BF16)
        back_q[2 * chunk] = q_grad[:, 0:BLOCK]
        back_q[2 * chunk + 1] = q_grad[:, BLOCK:]
        k_grad = dot(q_pair, dscore)
        kv_grad[0:H1] += (k_grad[0:H1] + k_grad[H1:H2]) * SCALE
        kv_grad[H1:H2] += dot(g_flat, prob.astype(BF16))
        for side in range(2):
            index = 2 * chunk + side
            mine = alone & (index == z_low)

            @pl.when(mine)
            def _():
                pltpu.make_async_copy(
                    back_q.at[index], got_q.at[z_low], bq_recv.at[z_low]
                ).start()

            @pl.when(jnp.logical_not(mine))
            def _():
                return_q(index).start()

        return carry

    lax.fori_loop(0, HALF // 2, attend, 0)

    def half_lanes(core):
        return pl.ds(pl.multiple_of(core * HALF * BLOCK, BLOCK), HALF * BLOCK)

    partial = pltpu.make_async_remote_copy(
        src_ref=kv_grad.at[:, half_lanes(1 - c)],
        dst_ref=kv_partial,
        send_sem=part_send,
        recv_sem=part_recv,
        device_id=core_peer,
    )
    partial.start()
    partial.wait_recv()

    def finish_kv(index, carry):
        mine_lanes = pl.ds(pl.multiple_of((HALF * c + index) * BLOCK, BLOCK), BLOCK)
        lanes = pl.ds(pl.multiple_of(index * BLOCK, BLOCK), BLOCK)
        back_kv[index] = (kv_grad[:, mine_lanes] + kv_partial[:, lanes]).astype(BF16)
        mine = alone & (index == z_low)

        @pl.when(mine)
        def _():
            pltpu.make_async_copy(
                back_kv.at[index], got_kv.at[z_low], bkv_recv.at[z_low]
            ).start()

        @pl.when(jnp.logical_not(mine))
        def _():
            return_kv(index).start()

        return carry

    lax.fori_loop(0, HALF, finish_kv, 0)

    total[...] = jnp.zeros_like(total)

    def combine(index, carry):
        q_block, kv_block = got_q.at[index], got_kv.at[index]
        pltpu.make_async_copy(q_block, q_block, bq_recv.at[index]).wait()
        pltpu.make_async_copy(kv_block, kv_block, bkv_recv.at[index]).wait()
        grads = jnp.concatenate([q_block[...], kv_block[...]], axis=0)
        total[...] += dot(flip(grads), weights[index, 0:H3])
        return carry

    lax.fori_loop(0, HALF, combine, 0)

    again = x_ref[...].astype(F32)
    rms = lax.rsqrt(jnp.mean(again * again, axis=-1, keepdims=True) + 1e-05)
    grad = total[...]
    branch_out[...] = (
        rms * grad - again * rms**3 * jnp.mean(grad * again, axis=-1, keepdims=True)
    ).astype(BF16)
    shift = pltpu.make_async_remote_copy(
        src_ref=branch_out,
        dst_ref=out_ref,
        send_sem=out_send,
        recv_sem=out_recv,
        device_id=before,
    )
    shift.start()

    for j in range(2):
        to_x(j).wait_send()
        to_core(j).wait_send()
        relay(j).wait_send()
    partial.wait_send()

    def drain(index, carry):
        kv_copy(index).wait_send()

        @pl.when(jnp.logical_not(alone & (index == z_low)))
        def _():
            send_copy(index).wait_send()
            return_q(index).wait_send()
            return_kv(index).wait_send()

        return carry

    lax.fori_loop(0, HALF, drain, 0)
    shift.wait()


def body(activations, out_grads, doc_ids, query_weight, key_weight, value_weight, out_weight):
    tokens = activations.shape[2]

    def by_head(weight):
        return weight[0].T.reshape(2, HEAD_DIM, WIDTH)

    weights = jnp.concatenate(
        [
            by_head(query_weight),
            by_head(key_weight),
            by_head(value_weight),
            out_weight[0].reshape(2, HEAD_DIM, WIDTH),
        ],
        axis=1,
    )
    doc_row = jnp.repeat(doc_ids, BLOCK, axis=1)[:, None, :]
    vmem = pl.BlockSpec(memory_space=pltpu.VMEM)
    dma = pltpu.SemaphoreType.DMA
    out = pl.pallas_call(
        kernel,
        out_shape=jax.ShapeDtypeStruct((tokens, WIDTH), BF16),
        in_specs=[
            pl.BlockSpec(memory_space=pltpu.SMEM),
            vmem,
            vmem,
            vmem,
            pl.BlockSpec(memory_space=pl.ANY),
        ],
        out_specs=vmem,
        scratch_shapes=[
            pltpu.VMEM((HALF, H4, WIDTH), BF16),
            pltpu.VMEM((BLOCK, WIDTH), BF16),
            pltpu.VMEM((HALF, H6, BLOCK), BF16),
            pltpu.VMEM((HALF, H6, BLOCK), BF16),
            pltpu.VMEM((HALF, H3, BLOCK), BF16),
            pltpu.VMEM((H3, N_CTX * BLOCK), BF16),
            pltpu.VMEM((H1, N_CTX * BLOCK), BF16),
            pltpu.VMEM((H2, N_CTX * BLOCK), F32),
            pltpu.VMEM((H2, HALF * BLOCK), F32),
            pltpu.VMEM((HALF, H1, BLOCK), BF16),
            pltpu.VMEM((HALF, H2, BLOCK), BF16),
            pltpu.VMEM((HALF, H1, BLOCK), BF16),
            pltpu.VMEM((HALF, H2, BLOCK), BF16),
            pltpu.VMEM((BLOCK, WIDTH), F32),
            pltpu.VMEM((BLOCK, WIDTH), BF16),
            dma((2, 2)),
            dma((2,)),
            dma((4, 2)),
            dma((HALF,)),
            dma((HALF,)),
            dma((HALF,)),
            dma((HALF,)),
            dma,
            dma,
            dma((HALF,)),
            dma((HALF,)),
            dma((HALF,)),
            dma((HALF,)),
            dma,
            dma,
        ],
        compiler_params=pltpu.CompilerParams(
            collective_id=0, has_side_effects=True, vmem_limit_bytes=48 * 2**20
        ),
    )(doc_ids, doc_row, activations[0, 0], out_grads[0, 0], weights)
    return out[None, None]


def solution(mesh):
    return jax.shard_map(
        body,
        mesh=mesh,
        in_specs=(
            P("section", "dp", "ctx", None),
            P("section", "dp", "ctx", None),
            P(),
            P("section", None, "dp"),
            P("section", None, "dp"),
            P("section", None, "dp"),
            P("section", "dp", None),
        ),
        out_specs=P("section", "dp", "ctx", None),
        check_vma=False,
    )
```

```python
import functools

import jax
import jax.numpy as jnp
from jax import lax
from jax.experimental import pallas as pl
from jax.experimental.pallas import tpu as pltpu
from jax.sharding import PartitionSpec as P

HEAD_DIM = 80
BLOCK = 128
WIDTH = 1280
N_CTX = 16
HALF = 8
SCALE = HEAD_DIM ** (-0.5)
NEG = -1e30
H1, H2, H3, H4, H6 = (n * HEAD_DIM for n in (1, 2, 3, 4, 6))
F32 = jnp.float32
BF16 = jnp.bfloat16
NT = (((1,), (1,)), ((), ()))


def dot(a, b):
    return jnp.dot(a, b, preferred_element_type=F32)


def dot_nt(a, b):
    return lax.dot_general(a, b, NT, preferred_element_type=F32)


def flip(matrix):
    return matrix.astype(F32).T.astype(BF16)


def split(wide):
    high = wide.astype(BF16)
    return high, (wide - high.astype(F32)).astype(BF16)


def kernel(
    docs_ref,
    x_ref,
    og_ref,
    wg_ref,
    w_ref,
    out_ref,
    acts,
    weights,
    send,
    recv,
    kv_other,
    keys3,
    values,
    doc_row,
    kv_grad,
    kv_partial,
    back_q,
    back_kv,
    got_q,
    got_kv,
    total,
    branch_out,
    own_sem,
    act_send,
    act_recv,
    w_send,
    w_recv,
    send_sem,
    recv_sem,
    kv_send,
    kv_recv,
    part_send,
    part_recv,
    bq_send,
    bq_recv,
    bkv_send,
    bkv_recv,
    out_send,
    out_recv,
):
    section = lax.axis_index("section")
    n_section = lax.axis_size("section")
    z = lax.axis_index("ctx")
    dp = lax.axis_index("dp")
    x, c = dp // 2, dp % 2
    z_half, z_low, page = z // HALF, z % HALF, z % 4
    core_peer = {"dp": 2 * x + 1 - c}
    x_peer = {"dp": 2 * (1 - x) + c}
    before = {"section": (section + n_section - 1) % n_section}
    after = {"section": (section + 1) % n_section}
    alone = z_half == c
    alone_back = alone & (page == dp)
    head = 4 * x + 2 * z_half + (z // 4) % 2

    def peer(index):
        return {"ctx": HALF * c + index, "dp": 2 * x + z_half}

    def peer_back(index):
        return {"ctx": HALF * c + index, "dp": page}

    def back_from(index):
        return {"ctx": HALF * ((index // 2) % 2) + 4 * (index % 2) + dp, "dp": 2 * (index // 4) + z_half}

    own_weights = pltpu.make_async_copy(w_ref, weights.at[dp], own_sem)
    own_weights.start()

    barrier = pltpu.get_barrier_semaphore()
    for other in (core_peer, x_peer, after):
        pl.semaphore_signal(barrier, inc=1, device_id=other)

    def greet(index, carry):
        @pl.when(jnp.logical_not(alone & (index == z_low)))
        def _():
            pl.semaphore_signal(barrier, inc=1, device_id=peer(index))

        @pl.when(jnp.logical_not(alone_back & (index == head)))
        def _():
            pl.semaphore_signal(barrier, inc=1, device_id=back_from(index))

        return carry

    lax.fori_loop(0, HALF, greet, 0)

    def page_of(r):
        return 2 * ((x + r // 2) % 2) + (c + r % 2) % 2

    def hand_on(buffer, r, target, send_ref, recv_ref):
        block = buffer.at[page_of(r)]
        return pltpu.make_async_remote_copy(
            src_ref=block, dst_ref=block, send_sem=send_ref, recv_sem=recv_ref, device_id=target
        )

    acts_to_x = hand_on(acts, 0, x_peer, act_send.at[0], act_recv.at[2])
    acts_to_core = hand_on(acts, 0, core_peer, act_send.at[1], act_recv.at[1])
    acts_relay = hand_on(acts, 2, core_peer, act_send.at[2], act_recv.at[3])
    weights_to_x = hand_on(weights, 0, x_peer, w_send.at[0], w_recv.at[2])
    weights_to_core = hand_on(weights, 0, core_peer, w_send.at[1], w_recv.at[1])
    weights_relay = hand_on(weights, 2, core_peer, w_send.at[2], w_recv.at[3])

    def here(buffer, r, recv_ref):
        block = buffer.at[page_of(r)]
        pltpu.make_async_copy(block, block, recv_ref.at[r]).wait()

    inputs = x_ref[...].astype(F32)
    inv_rms = lax.rsqrt(jnp.mean(inputs * inputs, axis=-1, keepdims=True) + 1e-05)
    acts[dp, 0:BLOCK] = (inputs * inv_rms).astype(BF16)
    acts[dp, BLOCK : 2 * BLOCK] = og_ref[...]
    for block in range(N_CTX):
        doc_row[:, block * BLOCK : (block + 1) * BLOCK] = jnp.full(
            (1, BLOCK), docs_ref[page, block], jnp.int32
        )

    pl.semaphore_wait(barrier, 19 - alone.astype(jnp.int32) - alone_back.astype(jnp.int32))
    acts_to_x.start()
    acts_to_core.start()
    own_weights.wait()

    def send_copy(index):
        return pltpu.make_async_remote_copy(
            src_ref=send.at[index],
            dst_ref=recv.at[z_low],
            send_sem=send_sem.at[index],
            recv_sem=recv_sem.at[z_low],
            device_id=peer(index),
        )

    def project(slot, j):
        qkv = dot_nt(weights[dp, j], acts[slot, 0:BLOCK])
        out_grad = dot_nt(wg_ref[j], acts[slot, BLOCK : 2 * BLOCK])
        q_high, q_low = split(qkv[0:H1])
        k_high, k_low = split(qkv[H1:H2])
        unit = 4 * j + slot
        message = send.at[unit]
        message[0:H1] = q_high
        message[H1:H2] = q_low
        message[H2:H3] = out_grad.astype(BF16)
        message[H3:H4] = k_high
        message[H4 : H4 + H1] = k_low
        message[H4 + H1 : H6] = qkv[H2:H3].astype(BF16)
        mine = alone & (unit == z_low)

        @pl.when(mine)
        def _():
            pltpu.make_async_copy(message, recv.at[z_low], recv_sem.at[z_low]).start()

        @pl.when(jnp.logical_not(mine))
        def _():
            send_copy(unit).start()

    def step(r, carry):
        @pl.when(r > 0)
        def _():
            here(acts, r, act_recv)

        @pl.when(r == 2)
        def _():
            acts_relay.start()
            weights_to_x.start()
            weights_to_core.start()

        project(page_of(r), 0)
        project(page_of(r), 1)
        return carry

    lax.fori_loop(0, 4, step, 0)

    def kv_copy(index):
        return pltpu.make_async_remote_copy(
            src_ref=recv.at[index, pl.ds(H3, H3)],
            dst_ref=kv_other.at[index],
            send_sem=kv_send.at[index],
            recv_sem=kv_recv.at[index],
            device_id=core_peer,
        )

    def place(block, kv):
        lanes = pl.ds(pl.multiple_of(block * BLOCK, BLOCK), BLOCK)
        keys3[0:H2, lanes] = kv[0:H2]
        keys3[H2:H3, lanes] = kv[0:H1]
        values[:, lanes] = kv[H2:H3]

    def arrive(index, carry):
        block = recv.at[index]
        pltpu.make_async_copy(block, block, recv_sem.at[index]).wait()
        kv_copy(index).start()
        place(HALF * c + index, recv[index, H3:H6])
        return carry

    lax.fori_loop(0, HALF, arrive, 0)

    def arrive_other(index, carry):
        kv_copy(index).wait_recv()
        place(HALF * (1 - c) + index, kv_other[index])
        return carry

    lax.fori_loop(0, HALF, arrive_other, 0)

    kv_grad[...] = jnp.zeros_like(kv_grad)

    def return_q(index):
        return pltpu.make_async_remote_copy(
            src_ref=back_q.at[index],
            dst_ref=got_q.at[head],
            send_sem=bq_send.at[index],
            recv_sem=bq_recv.at[head],
            device_id=peer_back(index),
        )

    def return_kv(index):
        return pltpu.make_async_remote_copy(
            src_ref=back_kv.at[index],
            dst_ref=got_kv.at[head],
            send_sem=bkv_send.at[index],
            recv_sem=bkv_recv.at[head],
            device_id=peer_back(index),
        )

    def attend(chunk, carry):
        one, two = recv.at[2 * chunk], recv.at[2 * chunk + 1]
        q_pair = jnp.concatenate([one[0:H2], two[0:H2]], axis=1)
        g_flat = jnp.concatenate([one[H2:H3], two[H2:H3]], axis=1)
        q3 = flip(jnp.concatenate([q_pair[0:H1], q_pair], axis=0))
        g = flip(g_flat)
        first = docs_ref[page, HALF * c + 2 * chunk]
        second = docs_ref[page, HALF * c + 2 * chunk + 1]
        rows = lax.broadcasted_iota(jnp.int32, (2 * BLOCK, 1), 0)
        allowed = jnp.where(rows < BLOCK, first, second) == doc_row[...]
        scores = jnp.where(allowed, dot(q3, keys3[...]) * SCALE, NEG)
        top = jnp.max(scores, axis=-1, keepdims=True)
        weight = jnp.exp(scores - top)
        share = 1.0 / jnp.sum(weight, axis=-1, keepdims=True)
        prob = weight * share
        dprob = dot(g, values[...])
        delta = jnp.sum(prob * dprob, axis=-1, keepdims=True)
        dscore = (prob * (dprob - delta)).astype(BF16)
        q_grad = dot_nt(keys3[0:H2], dscore)
        q_grad = ((q_grad[0:H1] + q_grad[H1:H2]) * SCALE).astype(BF16)
        back_q[2 * chunk] = q_grad[:, 0:BLOCK]
        back_q[2 * chunk + 1] = q_grad[:, BLOCK:]
        k_grad = dot(q_pair, dscore)
        kv_grad[0:H1] += (k_grad[0:H1] + k_grad[H1:H2]) * SCALE
        kv_grad[H1:H2] += dot(g_flat, prob.astype(BF16))
        for side in range(2):
            index = 2 * chunk + side
            mine = alone_back & (index == z_low)

            @pl.when(mine)
            def _():
                pltpu.make_async_copy(
                    back_q.at[index], got_q.at[head], bq_recv.at[head]
                ).start()

            @pl.when(jnp.logical_not(mine))
            def _():
                return_q(index).start()

        return carry

    lax.fori_loop(0, HALF // 2, attend, 0)

    def half_lanes(core):
        return pl.ds(pl.multiple_of(core * HALF * BLOCK, BLOCK), HALF * BLOCK)

    partial = pltpu.make_async_remote_copy(
        src_ref=kv_grad.at[:, half_lanes(1 - c)],
        dst_ref=kv_partial,
        send_sem=part_send,
        recv_sem=part_recv,
        device_id=core_peer,
    )
    partial.start()
    partial.wait_recv()

    def finish_kv(index, carry):
        mine_lanes = pl.ds(pl.multiple_of((HALF * c + index) * BLOCK, BLOCK), BLOCK)
        lanes = pl.ds(pl.multiple_of(index * BLOCK, BLOCK), BLOCK)
        back_kv[index] = (kv_grad[:, mine_lanes] + kv_partial[:, lanes]).astype(BF16)
        mine = alone_back & (index == z_low)

        @pl.when(mine)
        def _():
            pltpu.make_async_copy(
                back_kv.at[index], got_kv.at[head], bkv_recv.at[head]
            ).start()

        @pl.when(jnp.logical_not(mine))
        def _():
            return_kv(index).start()

        return carry

    lax.fori_loop(0, HALF, finish_kv, 0)

    here(weights, 1, w_recv)
    here(weights, 2, w_recv)
    weights_relay.start()
    total[...] = jnp.zeros_like(total)
    here(weights, 3, w_recv)

    def combine(index, carry):
        q_block, kv_block = got_q.at[index], got_kv.at[index]
        pltpu.make_async_copy(q_block, q_block, bq_recv.at[index]).wait()
        pltpu.make_async_copy(kv_block, kv_block, bkv_recv.at[index]).wait()
        grads = jnp.concatenate([q_block[...], kv_block[...]], axis=0)
        total[...] += dot(flip(grads), weights[index // 2, index % 2])
        return carry

    lax.fori_loop(0, HALF, combine, 0)

    again = x_ref[...].astype(F32)
    rms = lax.rsqrt(jnp.mean(again * again, axis=-1, keepdims=True) + 1e-05)
    grad = total[...]
    branch_out[...] = (
        rms * grad - again * rms**3 * jnp.mean(grad * again, axis=-1, keepdims=True)
    ).astype(BF16)
    shift = pltpu.make_async_remote_copy(
        src_ref=branch_out,
        dst_ref=out_ref,
        send_sem=out_send,
        recv_sem=out_recv,
        device_id=before,
    )
    shift.start()

    for sent in (acts_to_x, acts_to_core, acts_relay):
        sent.wait_send()
    for sent in (weights_to_x, weights_to_core, weights_relay):
        sent.wait_send()
    partial.wait_send()

    def drain(index, carry):
        kv_copy(index).wait_send()

        @pl.when(jnp.logical_not(alone & (index == z_low)))
        def _():
            send_copy(index).wait_send()

        @pl.when(jnp.logical_not(alone_back & (index == z_low)))
        def _():
            return_q(index).wait_send()
            return_kv(index).wait_send()

        return carry

    lax.fori_loop(0, HALF, drain, 0)
    shift.wait()


def body(activations, out_grads, doc_ids, query_weight, key_weight, value_weight, out_weight):
    tokens = activations.shape[2]

    def by_head(weight):
        return weight[0].T.reshape(2, HEAD_DIM, WIDTH)

    weights = jnp.concatenate(
        [by_head(query_weight), by_head(key_weight), by_head(value_weight)], axis=1
    )
    out_heads = out_weight[0].reshape(2, HEAD_DIM, WIDTH)
    vmem = pl.BlockSpec(memory_space=pltpu.VMEM)
    dma = pltpu.SemaphoreType.DMA
    out = pl.pallas_call(
        kernel,
        out_shape=jax.ShapeDtypeStruct((tokens, WIDTH), BF16),
        in_specs=[
            pl.BlockSpec(memory_space=pltpu.SMEM),
            vmem,
            vmem,
            vmem,
            pl.BlockSpec(memory_space=pl.ANY),
        ],
        out_specs=vmem,
        scratch_shapes=[
            pltpu.VMEM((4, 2 * BLOCK, WIDTH), BF16),
            pltpu.VMEM((4, 2, H3, WIDTH), BF16),
            pltpu.VMEM((HALF, H6, BLOCK), BF16),
            pltpu.VMEM((HALF, H6, BLOCK), BF16),
            pltpu.VMEM((HALF, H3, BLOCK), BF16),
            pltpu.VMEM((H3, N_CTX * BLOCK), BF16),
            pltpu.VMEM((H1, N_CTX * BLOCK), BF16),
            pltpu.VMEM((1, N_CTX * BLOCK), jnp.int32),
            pltpu.VMEM((H2, N_CTX * BLOCK), F32),
            pltpu.VMEM((H2, HALF * BLOCK), F32),
            pltpu.VMEM((HALF, H1, BLOCK), BF16),
            pltpu.VMEM((HALF, H2, BLOCK), BF16),
            pltpu.VMEM((HALF, H1, BLOCK), BF16),
            pltpu.VMEM((HALF, H2, BLOCK), BF16),
            pltpu.VMEM((BLOCK, WIDTH), F32),
            pltpu.VMEM((BLOCK, WIDTH), BF16),
            dma,
            dma((3,)),
            dma((4,)),
            dma((3,)),
            dma((4,)),
            dma((HALF,)),
            dma((HALF,)),
            dma((HALF,)),
            dma((HALF,)),
            dma,
            dma,
            dma((HALF,)),
            dma((HALF,)),
            dma((HALF,)),
            dma((HALF,)),
            dma,
            dma,
        ],
        compiler_params=pltpu.CompilerParams(
            collective_id=0, has_side_effects=True, vmem_limit_bytes=48 * 2**20
        ),
    )(doc_ids, activations[0, 0], out_grads[0, 0], out_heads, weights)
    return out[None, None]


def solution(mesh):
    return jax.shard_map(
        body,
        mesh=mesh,
        in_specs=(
            P("section", "dp", "ctx", None),
            P("section", "dp", "ctx", None),
            P(),
            P("section", None, "dp"),
            P("section", None, "dp"),
            P("section", None, "dp"),
            P("section", "dp", None),
        ),
        out_specs=P("section", "dp", "ctx", None),
        check_vma=False,
    )
```

```python
import functools

import jax
import jax.numpy as jnp
from jax import lax
from jax.experimental import pallas as pl
from jax.experimental.pallas import tpu as pltpu
from jax.sharding import PartitionSpec as P

HEAD_DIM = 80
BLOCK = 128
WIDTH = 1280
N_CTX = 16
HALF = 8
SCALE = HEAD_DIM ** (-0.5)
NEG = -1e30
H1, H2, H3, H4, H6 = (n * HEAD_DIM for n in (1, 2, 3, 4, 6))
F32 = jnp.float32
BF16 = jnp.bfloat16
NT = (((1,), (1,)), ((), ()))


def dot(a, b):
    return jnp.dot(a, b, preferred_element_type=F32)


def dot_nt(a, b):
    return lax.dot_general(a, b, NT, preferred_element_type=F32)


def flip(matrix):
    return matrix.astype(F32).T.astype(BF16)


def split(wide):
    high = wide.astype(BF16)
    return high, (wide - high.astype(F32)).astype(BF16)


def kernel(
    docs_ref,
    x_hbm,
    og_hbm,
    wq_hbm,
    wk_hbm,
    wv_hbm,
    wg_hbm,
    out_ref,
    x_ref,
    wg_ref,
    acts,
    weights,
    send,
    recv,
    kv_other,
    keys3,
    values,
    kv_grad,
    kv_partial,
    back_q,
    back_kv,
    got_q,
    got_kv,
    total,
    branch_out,
    load_sem,
    act_send,
    act_recv,
    w_send,
    w_recv,
    send_sem,
    recv_sem,
    kv_send,
    kv_recv,
    part_send,
    part_recv,
    bq_send,
    bq_recv,
    bkv_send,
    bkv_recv,
    out_send,
    out_recv,
):
    section = lax.axis_index("section")
    n_section = lax.axis_size("section")
    z = lax.axis_index("ctx")
    dp = lax.axis_index("dp")
    x, c = dp // 2, dp % 2
    z_half, z_low, page = z // HALF, z % HALF, z % 4
    core_peer = {"dp": 2 * x + 1 - c}
    x_peer = {"dp": 2 * (1 - x) + c}
    before = {"section": (section + n_section - 1) % n_section}
    after = {"section": (section + 1) % n_section}
    alone = z_half == c
    alone_back = alone & (page == dp)
    late = page // 2 != x
    head = 4 * x + 2 * z_half + (z // 4) % 2

    def peer(index):
        return {"ctx": HALF * c + index, "dp": 2 * x + z_half}

    def peer_back(index):
        return {"ctx": HALF * c + index, "dp": page}

    def back_from(index):
        return {"ctx": HALF * ((index // 2) % 2) + 4 * (index % 2) + dp, "dp": 2 * (index // 4) + z_half}

    barrier = pltpu.get_barrier_semaphore()
    for other in (core_peer, x_peer, after):
        pl.semaphore_signal(barrier, inc=1, device_id=other)

    def greet(index, carry):
        @pl.when(jnp.logical_not(alone & (index == z_low)))
        def _():
            pl.semaphore_signal(barrier, inc=1, device_id=peer(index))

        @pl.when(jnp.logical_not(alone_back & (index == head)))
        def _():
            pl.semaphore_signal(barrier, inc=1, device_id=back_from(index))

        return carry

    lax.fori_loop(0, HALF, greet, 0)

    loads = [
        pltpu.make_async_copy(source, target, load_sem.at[number])
        for number, (source, target) in enumerate(
            (
                (x_hbm, x_ref),
                (wq_hbm, weights.at[dp, :, pl.ds(0, H1)]),
                (wk_hbm, weights.at[dp, :, pl.ds(H1, H1)]),
                (wv_hbm, weights.at[dp, :, pl.ds(H2, H1)]),
                (og_hbm, acts.at[dp, pl.ds(BLOCK, BLOCK)]),
                (wg_hbm, wg_ref),
            )
        )
    ]
    for load in loads:
        load.start()

    rows = lax.broadcasted_iota(jnp.int32, (16, BLOCK), 0)
    for block in range(N_CTX):
        keys3[H3 : H3 + 16, block * BLOCK : (block + 1) * BLOCK] = jnp.where(
            (rows == docs_ref[page, block]) | (rows >= 4), 0.0, NEG
        ).astype(BF16)

    def page_of(r):
        return 2 * ((x + r // 2) % 2) + (c + r % 2) % 2

    def hand_on(buffer, r, target, send_ref, recv_ref):
        block = buffer.at[page_of(r)]
        return pltpu.make_async_remote_copy(
            src_ref=block, dst_ref=block, send_sem=send_ref, recv_sem=recv_ref, device_id=target
        )

    acts_to_x = hand_on(acts, 0, x_peer, act_send.at[0], act_recv.at[2])
    acts_to_core = hand_on(acts, 0, core_peer, act_send.at[1], act_recv.at[1])
    acts_relay = hand_on(acts, 2, core_peer, act_send.at[2], act_recv.at[3])
    weights_to_x = hand_on(weights, 0, x_peer, w_send.at[0], w_recv.at[2])
    weights_to_core = hand_on(weights, 0, core_peer, w_send.at[1], w_recv.at[1])
    weights_relay = hand_on(weights, 2, core_peer, w_send.at[2], w_recv.at[3])

    def here(buffer, r, recv_ref):
        block = buffer.at[page_of(r)]
        pltpu.make_async_copy(block, block, recv_ref.at[r]).wait()

    loads[0].wait()
    inputs = x_ref[...].astype(F32)
    inv_rms = lax.rsqrt(jnp.mean(inputs * inputs, axis=-1, keepdims=True) + 1e-05)
    acts[dp, 0:BLOCK] = (inputs * inv_rms).astype(BF16)
    for load in loads[1:]:
        load.wait()

    def send_copy(index):
        return pltpu.make_async_remote_copy(
            src_ref=send.at[index],
            dst_ref=recv.at[z_low],
            send_sem=send_sem.at[index],
            recv_sem=recv_sem.at[z_low],
            device_id=peer(index),
        )

    def project(slot, j):
        qkv = dot_nt(weights[dp, j], acts[slot, 0:BLOCK])
        out_grad = dot_nt(wg_ref[j], acts[slot, BLOCK : 2 * BLOCK])
        q_high, q_low = split(qkv[0:H1] * SCALE)
        k_high, k_low = split(qkv[H1:H2])
        unit = 4 * j + slot
        message = send.at[unit]
        message[0:H1] = q_high
        message[H1:H2] = q_low
        message[H2:H3] = out_grad.astype(BF16)
        message[H3:H4] = k_high
        message[H4 : H4 + H1] = k_low
        message[H4 + H1 : H6] = qkv[H2:H3].astype(BF16)

    def dispatch(unit):
        message = send.at[unit]
        mine = alone & (unit == z_low)

        @pl.when(mine)
        def _():
            pltpu.make_async_copy(message, recv.at[z_low], recv_sem.at[z_low]).start()

        @pl.when(jnp.logical_not(mine))
        def _():
            send_copy(unit).start()

    project(dp, 0)
    project(dp, 1)
    pl.semaphore_wait(barrier, 19 - alone.astype(jnp.int32) - alone_back.astype(jnp.int32))
    acts_to_x.start()
    acts_to_core.start()
    dispatch(dp)
    dispatch(4 + dp)

    def step(r, carry):
        here(acts, r, act_recv)

        @pl.when(r == 2)
        def _():
            acts_relay.start()
            weights_to_x.start()
            weights_to_core.start()

        for j in range(2):
            project(page_of(r), j)
            dispatch(4 * j + page_of(r))
        return carry

    lax.fori_loop(1, 4, step, 0)

    def kv_copy(index):
        return pltpu.make_async_remote_copy(
            src_ref=recv.at[index, pl.ds(H3, H3)],
            dst_ref=kv_other.at[index],
            send_sem=kv_send.at[index],
            recv_sem=kv_recv.at[index],
            device_id=core_peer,
        )

    def place(block, kv):
        lanes = pl.ds(pl.multiple_of(block * BLOCK, BLOCK), BLOCK)
        keys3[0:H2, lanes] = kv[0:H2]
        keys3[H2:H3, lanes] = kv[0:H1]
        values[:, lanes] = kv[H2:H3]

    def arrive(index, carry):
        block = recv.at[index]
        pltpu.make_async_copy(block, block, recv_sem.at[index]).wait()
        kv_copy(index).start()
        place(HALF * c + index, recv[index, H3:H6])
        return carry

    lax.fori_loop(0, HALF, arrive, 0)

    def arrive_other(index, carry):
        kv_copy(index).wait_recv()
        place(HALF * (1 - c) + index, kv_other[index])
        return carry

    lax.fori_loop(0, HALF, arrive_other, 0)

    kv_grad[...] = jnp.zeros_like(kv_grad)

    def return_q(index):
        return pltpu.make_async_remote_copy(
            src_ref=back_q.at[index],
            dst_ref=got_q.at[head],
            send_sem=bq_send.at[index],
            recv_sem=bq_recv.at[head],
            device_id=peer_back(index),
        )

    def return_kv(index):
        return pltpu.make_async_remote_copy(
            src_ref=back_kv.at[index],
            dst_ref=got_kv.at[head],
            send_sem=bkv_send.at[index],
            recv_sem=bkv_recv.at[head],
            device_id=peer_back(index),
        )

    def give_q(index):
        mine = alone_back & (index == z_low)

        @pl.when(mine)
        def _():
            pltpu.make_async_copy(back_q.at[index], got_q.at[head], bq_recv.at[head]).start()

        @pl.when(jnp.logical_not(mine))
        def _():
            return_q(index).start()

    def in_order(step, count):
        return c * (count - 1) + (1 - 2 * c) * step

    def attend(step, carry):
        chunk = in_order(step, HALF // 2)
        one, two = recv.at[2 * chunk], recv.at[2 * chunk + 1]
        q_pair = jnp.concatenate([one[0:H2], two[0:H2]], axis=1)
        g_flat = jnp.concatenate([one[H2:H3], two[H2:H3]], axis=1)
        g = flip(g_flat)
        first = docs_ref[page, HALF * c + 2 * chunk]
        second = docs_ref[page, HALF * c + 2 * chunk + 1]
        shape = (16, 2 * BLOCK)
        lanes = lax.broadcasted_iota(jnp.int32, shape, 1)
        document = jnp.where(lanes < BLOCK, first, second)
        which = (lax.broadcasted_iota(jnp.int32, shape, 0) == document).astype(F32).astype(BF16)
        q3 = flip(jnp.concatenate([q_pair[0:H1], q_pair, which], axis=0))
        scores = dot(q3, keys3[...])
        top = jnp.max(scores, axis=-1, keepdims=True)
        weight = jnp.exp(scores - top)
        share = 1.0 / jnp.sum(weight, axis=-1, keepdims=True)
        prob = weight * share
        dprob = dot(g, values[...])
        delta = jnp.sum(prob * dprob, axis=-1, keepdims=True)
        dscore = (prob * (dprob - delta)).astype(BF16)
        q_grad = dot_nt(keys3[0:H2], dscore)
        q_grad = ((q_grad[0:H1] + q_grad[H1:H2]) * SCALE).astype(BF16)
        back_q[2 * chunk] = q_grad[:, 0:BLOCK]
        back_q[2 * chunk + 1] = q_grad[:, BLOCK:]
        k_grad = dot(q_pair, dscore)
        kv_grad[0:H1] += k_grad[0:H1] + k_grad[H1:H2]
        kv_grad[H1:H2] += dot(g_flat, prob.astype(BF16))
        @pl.when(late)
        def _():
            give_q(2 * chunk + c)
            give_q(2 * chunk + 1 - c)

        return carry

    lax.fori_loop(0, HALF // 2, attend, 0)

    def half_lanes(core):
        return pl.ds(pl.multiple_of(core * HALF * BLOCK, BLOCK), HALF * BLOCK)

    partial = pltpu.make_async_remote_copy(
        src_ref=kv_grad.at[:, half_lanes(1 - c)],
        dst_ref=kv_partial,
        send_sem=part_send,
        recv_sem=part_recv,
        device_id=core_peer,
    )
    partial.start()
    partial.wait_recv()

    def sent_all(index, carry):
        @pl.when(jnp.logical_not(alone & (index == z_low)))
        def _():
            send_copy(index).wait_send()

        return carry

    lax.fori_loop(0, HALF, sent_all, 0)

    def finish_kv(step, carry):
        index = in_order(step, HALF)

        @pl.when(jnp.logical_not(late))
        def _():
            give_q(index)

        mine_lanes = pl.ds(pl.multiple_of((HALF * c + index) * BLOCK, BLOCK), BLOCK)
        lanes = pl.ds(pl.multiple_of(index * BLOCK, BLOCK), BLOCK)
        back_kv[index] = (kv_grad[:, mine_lanes] + kv_partial[:, lanes]).astype(BF16)
        mine = alone_back & (index == z_low)

        @pl.when(mine)
        def _():
            pltpu.make_async_copy(
                back_kv.at[index], got_kv.at[head], bkv_recv.at[head]
            ).start()

        @pl.when(jnp.logical_not(mine))
        def _():
            return_kv(index).start()

        return carry

    lax.fori_loop(0, HALF, finish_kv, 0)

    here(weights, 1, w_recv)
    here(weights, 2, w_recv)
    weights_relay.start()
    total[...] = jnp.zeros_like(total)
    here(weights, 3, w_recv)

    def combine(step, carry):
        index = (4 * x + step) % HALF
        q_block, kv_block = got_q.at[index], got_kv.at[index]
        pltpu.make_async_copy(q_block, q_block, bq_recv.at[index]).wait()
        pltpu.make_async_copy(kv_block, kv_block, bkv_recv.at[index]).wait()
        grads = jnp.concatenate([q_block[...], kv_block[...]], axis=0)
        total[...] += dot(flip(grads), weights[index // 2, index % 2])
        return carry

    lax.fori_loop(0, HALF, combine, 0)

    again = x_ref[...].astype(F32)
    rms = lax.rsqrt(jnp.mean(again * again, axis=-1, keepdims=True) + 1e-05)
    grad = total[...]
    branch_out[...] = (
        rms * grad - again * rms**3 * jnp.mean(grad * again, axis=-1, keepdims=True)
    ).astype(BF16)
    shift = pltpu.make_async_remote_copy(
        src_ref=branch_out,
        dst_ref=out_ref,
        send_sem=out_send,
        recv_sem=out_recv,
        device_id=before,
    )
    shift.start()

    for sent in (acts_to_x, acts_to_core, acts_relay):
        sent.wait_send()
    for sent in (weights_to_x, weights_to_core, weights_relay):
        sent.wait_send()
    partial.wait_send()

    def drain(index, carry):
        kv_copy(index).wait_send()

        @pl.when(jnp.logical_not(alone_back & (index == z_low)))
        def _():
            return_q(index).wait_send()
            return_kv(index).wait_send()

        return carry

    lax.fori_loop(0, HALF, drain, 0)
    shift.wait()


def body(activations, out_grads, doc_ids, query_weight, key_weight, value_weight, out_weight):
    tokens = activations.shape[2]

    def stay(array):
        return pltpu.with_memory_space_constraint(array, pltpu.HBM)

    def by_head(rows):
        return stay(rows.reshape(2, HEAD_DIM, WIDTH))

    anywhere = pl.BlockSpec(memory_space=pl.ANY)
    vmem = pl.BlockSpec(memory_space=pltpu.VMEM)
    dma = pltpu.SemaphoreType.DMA
    out = pl.pallas_call(
        kernel,
        out_shape=jax.ShapeDtypeStruct((tokens, WIDTH), BF16),
        in_specs=[pl.BlockSpec(memory_space=pltpu.SMEM)] + [anywhere] * 6,
        out_specs=vmem,
        scratch_shapes=[
            pltpu.VMEM((BLOCK, WIDTH), BF16),
            pltpu.VMEM((2, HEAD_DIM, WIDTH), BF16),
            pltpu.VMEM((4, 2 * BLOCK, WIDTH), BF16),
            pltpu.VMEM((4, 2, H3, WIDTH), BF16),
            pltpu.VMEM((HALF, H6, BLOCK), BF16),
            pltpu.VMEM((HALF, H6, BLOCK), BF16),
            pltpu.VMEM((HALF, H3, BLOCK), BF16),
            pltpu.VMEM((H3 + 16, N_CTX * BLOCK), BF16),
            pltpu.VMEM((H1, N_CTX * BLOCK), BF16),
            pltpu.VMEM((H2, N_CTX * BLOCK), F32),
            pltpu.VMEM((H2, HALF * BLOCK), F32),
            pltpu.VMEM((HALF, H1, BLOCK), BF16),
            pltpu.VMEM((HALF, H2, BLOCK), BF16),
            pltpu.VMEM((HALF, H1, BLOCK), BF16),
            pltpu.VMEM((HALF, H2, BLOCK), BF16),
            pltpu.VMEM((BLOCK, WIDTH), F32),
            pltpu.VMEM((BLOCK, WIDTH), BF16),
            dma((6,)),
            dma((3,)),
            dma((4,)),
            dma((3,)),
            dma((4,)),
            dma((HALF,)),
            dma((HALF,)),
            dma((HALF,)),
            dma((HALF,)),
            dma,
            dma,
            dma((HALF,)),
            dma((HALF,)),
            dma((HALF,)),
            dma((HALF,)),
            dma,
            dma,
        ],
        compiler_params=pltpu.CompilerParams(
            collective_id=0, has_side_effects=True, vmem_limit_bytes=48 * 2**20
        ),
    )(
        doc_ids,
        stay(activations[0, 0]),
        stay(out_grads[0, 0]),
        by_head(query_weight[0].T),
        by_head(key_weight[0].T),
        by_head(value_weight[0].T),
        by_head(out_weight[0]),
    )
    return out[None, None]


def solution(mesh):
    return jax.shard_map(
        body,
        mesh=mesh,
        in_specs=(
            P("section", "dp", "ctx", None),
            P("section", "dp", "ctx", None),
            P(),
            P("section", None, "dp"),
            P("section", None, "dp"),
            P("section", None, "dp"),
            P("section", "dp", None),
        ),
        out_specs=P("section", "dp", "ctx", None),
        check_vma=False,
    )
```

```python
import functools

import jax
import jax.numpy as jnp
from jax import lax
from jax.experimental import pallas as pl
from jax.experimental.pallas import tpu as pltpu
from jax.sharding import PartitionSpec as P

HEAD_DIM = 80
BLOCK = 128
WIDTH = 1280
N_CTX = 16
HALF = 8
SCALE = HEAD_DIM ** (-0.5)
NEG = -1e30
H1, H2, H3, H4, H6 = (n * HEAD_DIM for n in (1, 2, 3, 4, 6))
F32 = jnp.float32
BF16 = jnp.bfloat16
NT = (((1,), (1,)), ((), ()))


def dot(a, b):
    return jnp.dot(a, b, preferred_element_type=F32)


def dot_nt(a, b):
    return lax.dot_general(a, b, NT, preferred_element_type=F32)


def swap(two_bits):
    return 2 * (two_bits % 2) + two_bits // 2


def flip(matrix):
    return matrix.astype(F32).T.astype(BF16)


def split(wide):
    high = wide.astype(BF16)
    return high, (wide - high.astype(F32)).astype(BF16)


def kernel(
    docs_ref,
    x_hbm,
    og_hbm,
    wq_hbm,
    wk_hbm,
    wv_hbm,
    wg_hbm,
    out_ref,
    x_ref,
    wg_ref,
    acts,
    weights,
    send,
    recv,
    kv_other,
    keys3,
    values,
    kv_grad,
    kv_partial,
    back_q,
    back_kv,
    got_q,
    got_kv,
    total,
    branch_out,
    load_sem,
    act_send,
    act_recv,
    w_send,
    w_recv,
    send_sem,
    recv_sem,
    kv_send,
    kv_recv,
    part_send,
    part_recv,
    bq_send,
    bq_recv,
    bkv_send,
    bkv_recv,
    out_send,
    out_recv,
):
    section = lax.axis_index("section")
    n_section = lax.axis_size("section")
    z = lax.axis_index("ctx")
    dp = lax.axis_index("dp")
    x, c = dp // 2, dp % 2
    z_half, z_low, page = z // HALF, z % HALF, swap(z % 4)
    core_peer = {"dp": 2 * x + 1 - c}
    x_peer = {"dp": 2 * (1 - x) + c}
    before = {"section": (section + n_section - 1) % n_section}
    after = {"section": (section + 1) % n_section}
    alone = z_half == c
    alone_back = alone & (page == dp)
    late = page // 2 != x
    head = 4 * x + 2 * z_half + (z // 4) % 2

    def peer(index):
        return {"ctx": HALF * c + index, "dp": 2 * x + z_half}

    def peer_back(index):
        return {"ctx": HALF * c + index, "dp": page}

    def back_from(index):
        return {"ctx": HALF * ((index // 2) % 2) + 4 * (index % 2) + swap(dp), "dp": 2 * (index // 4) + z_half}

    barrier = pltpu.get_barrier_semaphore()
    for other in (core_peer, x_peer, after):
        pl.semaphore_signal(barrier, inc=1, device_id=other)

    def greet(index, carry):
        @pl.when(jnp.logical_not(alone & (index == z_low)))
        def _():
            pl.semaphore_signal(barrier, inc=1, device_id=peer(index))

        @pl.when(jnp.logical_not(alone_back & (index == head)))
        def _():
            pl.semaphore_signal(barrier, inc=1, device_id=back_from(index))

        return carry

    lax.fori_loop(0, HALF, greet, 0)

    loads = [
        pltpu.make_async_copy(source, target, load_sem.at[number])
        for number, (source, target) in enumerate(
            (
                (x_hbm, x_ref),
                (wq_hbm, weights.at[dp, :, pl.ds(0, H1)]),
                (wk_hbm, weights.at[dp, :, pl.ds(H1, H1)]),
                (wv_hbm, weights.at[dp, :, pl.ds(H2, H1)]),
                (og_hbm, acts.at[dp, pl.ds(BLOCK, BLOCK)]),
                (wg_hbm, wg_ref),
            )
        )
    ]
    for load in loads:
        load.start()

    rows = lax.broadcasted_iota(jnp.int32, (16, BLOCK), 0)
    for block in range(N_CTX):
        keys3[H3 : H3 + 16, block * BLOCK : (block + 1) * BLOCK] = jnp.where(
            (rows == docs_ref[page, block]) | (rows >= 4), 0.0, NEG
        ).astype(BF16)

    def page_of(r):
        return 2 * ((x + r // 2) % 2) + (c + r % 2) % 2

    def hand_on(buffer, r, target, send_ref, recv_ref):
        block = buffer.at[page_of(r)]
        return pltpu.make_async_remote_copy(
            src_ref=block, dst_ref=block, send_sem=send_ref, recv_sem=recv_ref, device_id=target
        )

    acts_to_x = hand_on(acts, 0, x_peer, act_send.at[0], act_recv.at[2])
    acts_to_core = hand_on(acts, 0, core_peer, act_send.at[1], act_recv.at[1])
    acts_relay = hand_on(acts, 2, core_peer, act_send.at[2], act_recv.at[3])
    weights_to_x = hand_on(weights, 0, x_peer, w_send.at[0], w_recv.at[2])
    weights_to_core = hand_on(weights, 0, core_peer, w_send.at[1], w_recv.at[1])
    weights_relay = hand_on(weights, 2, core_peer, w_send.at[2], w_recv.at[3])

    def here(buffer, r, recv_ref):
        block = buffer.at[page_of(r)]
        pltpu.make_async_copy(block, block, recv_ref.at[r]).wait()

    loads[0].wait()
    inputs = x_ref[...].astype(F32)
    inv_rms = lax.rsqrt(jnp.mean(inputs * inputs, axis=-1, keepdims=True) + 1e-05)
    acts[dp, 0:BLOCK] = (inputs * inv_rms).astype(BF16)
    for load in loads[1:]:
        load.wait()

    def send_copy(index):
        return pltpu.make_async_remote_copy(
            src_ref=send.at[index],
            dst_ref=recv.at[z_low],
            send_sem=send_sem.at[index],
            recv_sem=recv_sem.at[z_low],
            device_id=peer(index),
        )

    def project(slot, j):
        qkv = dot_nt(weights[dp, j], acts[slot, 0:BLOCK])
        out_grad = dot_nt(wg_ref[j], acts[slot, BLOCK : 2 * BLOCK])
        q_high, q_low = split(qkv[0:H1] * SCALE)
        k_high, k_low = split(qkv[H1:H2])
        unit = 4 * j + swap(slot)
        message = send.at[unit]
        message[0:H1] = q_high
        message[H1:H2] = q_low
        message[H2:H3] = out_grad.astype(BF16)
        message[H3:H4] = k_high
        message[H4 : H4 + H1] = k_low
        message[H4 + H1 : H6] = qkv[H2:H3].astype(BF16)

    def dispatch(unit):
        message = send.at[unit]
        mine = alone & (unit == z_low)

        @pl.when(mine)
        def _():
            pltpu.make_async_copy(message, recv.at[z_low], recv_sem.at[z_low]).start()

        @pl.when(jnp.logical_not(mine))
        def _():
            send_copy(unit).start()

    project(dp, 0)
    project(dp, 1)
    pl.semaphore_wait(barrier, 19 - alone.astype(jnp.int32) - alone_back.astype(jnp.int32))
    acts_to_x.start()
    acts_to_core.start()
    dispatch(swap(dp))
    dispatch(4 + swap(dp))

    def step(r, carry):
        here(acts, r, act_recv)

        @pl.when(r == 2)
        def _():
            acts_relay.start()
            weights_to_x.start()
            weights_to_core.start()

        for j in range(2):
            project(page_of(r), j)
            dispatch(4 * j + swap(page_of(r)))
        return carry

    lax.fori_loop(1, 4, step, 0)

    def kv_copy(index):
        return pltpu.make_async_remote_copy(
            src_ref=recv.at[index, pl.ds(H3, H3)],
            dst_ref=kv_other.at[index],
            send_sem=kv_send.at[index],
            recv_sem=kv_recv.at[index],
            device_id=core_peer,
        )

    def place(block, kv):
        lanes = pl.ds(pl.multiple_of(block * BLOCK, BLOCK), BLOCK)
        keys3[0:H2, lanes] = kv[0:H2]
        keys3[H2:H3, lanes] = kv[0:H1]
        values[:, lanes] = kv[H2:H3]

    def arrive(index, carry):
        block = recv.at[index]
        pltpu.make_async_copy(block, block, recv_sem.at[index]).wait()
        kv_copy(index).start()
        place(HALF * c + index, recv[index, H3:H6])
        return carry

    lax.fori_loop(0, HALF, arrive, 0)

    def arrive_other(index, carry):
        kv_copy(index).wait_recv()
        place(HALF * (1 - c) + index, kv_other[index])
        return carry

    lax.fori_loop(0, HALF, arrive_other, 0)

    kv_grad[...] = jnp.zeros_like(kv_grad)

    def return_q(index):
        return pltpu.make_async_remote_copy(
            src_ref=back_q.at[index],
            dst_ref=got_q.at[head],
            send_sem=bq_send.at[index],
            recv_sem=bq_recv.at[head],
            device_id=peer_back(index),
        )

    def return_kv(index):
        return pltpu.make_async_remote_copy(
            src_ref=back_kv.at[index],
            dst_ref=got_kv.at[head],
            send_sem=bkv_send.at[index],
            recv_sem=bkv_recv.at[head],
            device_id=peer_back(index),
        )

    def give_q(index):
        mine = alone_back & (index == z_low)

        @pl.when(mine)
        def _():
            pltpu.make_async_copy(back_q.at[index], got_q.at[head], bq_recv.at[head]).start()

        @pl.when(jnp.logical_not(mine))
        def _():
            return_q(index).start()

    def in_order(step, count):
        return c * (count - 1) + (1 - 2 * c) * step

    def attend(step, carry):
        chunk = in_order(step, HALF // 2)
        one, two = recv.at[2 * chunk], recv.at[2 * chunk + 1]
        q_pair = jnp.concatenate([one[0:H2], two[0:H2]], axis=1)
        g_flat = jnp.concatenate([one[H2:H3], two[H2:H3]], axis=1)
        g = flip(g_flat)
        first = docs_ref[page, HALF * c + 2 * chunk]
        second = docs_ref[page, HALF * c + 2 * chunk + 1]
        shape = (16, 2 * BLOCK)
        lanes = lax.broadcasted_iota(jnp.int32, shape, 1)
        document = jnp.where(lanes < BLOCK, first, second)
        which = (lax.broadcasted_iota(jnp.int32, shape, 0) == document).astype(F32).astype(BF16)
        q3 = flip(jnp.concatenate([q_pair[0:H1], q_pair, which], axis=0))
        scores = dot(q3, keys3[...])
        top = jnp.max(scores, axis=-1, keepdims=True)
        weight = jnp.exp(scores - top)
        share = 1.0 / jnp.sum(weight, axis=-1, keepdims=True)
        prob = weight * share
        dprob = dot(g, values[...])
        delta = jnp.sum(prob * dprob, axis=-1, keepdims=True)
        dscore = (prob * (dprob - delta)).astype(BF16)
        q_grad = dot_nt(keys3[0:H2], dscore)
        q_grad = ((q_grad[0:H1] + q_grad[H1:H2]) * SCALE).astype(BF16)
        back_q[2 * chunk] = q_grad[:, 0:BLOCK]
        back_q[2 * chunk + 1] = q_grad[:, BLOCK:]
        k_grad = dot(q_pair, dscore)
        kv_grad[0:H1] += k_grad[0:H1] + k_grad[H1:H2]
        kv_grad[H1:H2] += dot(g_flat, prob.astype(BF16))
        if True:
            give_q(2 * chunk + c)
            give_q(2 * chunk + 1 - c)

        return carry

    lax.fori_loop(0, HALF // 2, attend, 0)

    def half_lanes(core):
        return pl.ds(pl.multiple_of(core * HALF * BLOCK, BLOCK), HALF * BLOCK)

    partial = pltpu.make_async_remote_copy(
        src_ref=kv_grad.at[:, half_lanes(1 - c)],
        dst_ref=kv_partial,
        send_sem=part_send,
        recv_sem=part_recv,
        device_id=core_peer,
    )
    partial.start()
    partial.wait_recv()

    def sent_all(index, carry):
        @pl.when(jnp.logical_not(alone & (index == z_low)))
        def _():
            send_copy(index).wait_send()

        return carry

    lax.fori_loop(0, HALF, sent_all, 0)

    def finish_kv(step, carry):
        index = in_order(step, HALF)

        mine_lanes = pl.ds(pl.multiple_of((HALF * c + index) * BLOCK, BLOCK), BLOCK)
        lanes = pl.ds(pl.multiple_of(index * BLOCK, BLOCK), BLOCK)
        back_kv[index] = (kv_grad[:, mine_lanes] + kv_partial[:, lanes]).astype(BF16)
        mine = alone_back & (index == z_low)

        @pl.when(mine)
        def _():
            pltpu.make_async_copy(
                back_kv.at[index], got_kv.at[head], bkv_recv.at[head]
            ).start()

        @pl.when(jnp.logical_not(mine))
        def _():
            return_kv(index).start()

        return carry

    lax.fori_loop(0, HALF, finish_kv, 0)

    here(weights, 1, w_recv)
    here(weights, 2, w_recv)
    weights_relay.start()
    total[...] = jnp.zeros_like(total)
    here(weights, 3, w_recv)

    def combine(step, carry):
        index = (4 * x + step) % HALF
        q_block, kv_block = got_q.at[index], got_kv.at[index]
        pltpu.make_async_copy(q_block, q_block, bq_recv.at[index]).wait()
        pltpu.make_async_copy(kv_block, kv_block, bkv_recv.at[index]).wait()
        grads = jnp.concatenate([q_block[...], kv_block[...]], axis=0)
        total[...] += dot(flip(grads), weights[index // 2, index % 2])
        return carry

    lax.fori_loop(0, HALF, combine, 0)

    again = x_ref[...].astype(F32)
    rms = lax.rsqrt(jnp.mean(again * again, axis=-1, keepdims=True) + 1e-05)
    grad = total[...]
    branch_out[...] = (
        rms * grad - again * rms**3 * jnp.mean(grad * again, axis=-1, keepdims=True)
    ).astype(BF16)
    shift = pltpu.make_async_remote_copy(
        src_ref=branch_out,
        dst_ref=out_ref,
        send_sem=out_send,
        recv_sem=out_recv,
        device_id=before,
    )
    shift.start()

    for sent in (acts_to_x, acts_to_core, acts_relay):
        sent.wait_send()
    for sent in (weights_to_x, weights_to_core, weights_relay):
        sent.wait_send()
    partial.wait_send()

    def drain(index, carry):
        kv_copy(index).wait_send()

        @pl.when(jnp.logical_not(alone_back & (index == z_low)))
        def _():
            return_q(index).wait_send()
            return_kv(index).wait_send()

        return carry

    lax.fori_loop(0, HALF, drain, 0)
    shift.wait()


def body(activations, out_grads, doc_ids, query_weight, key_weight, value_weight, out_weight):
    tokens = activations.shape[2]

    def stay(array):
        return pltpu.with_memory_space_constraint(array, pltpu.HBM)

    def by_head(rows):
        return stay(rows.reshape(2, HEAD_DIM, WIDTH))

    anywhere = pl.BlockSpec(memory_space=pl.ANY)
    vmem = pl.BlockSpec(memory_space=pltpu.VMEM)
    dma = pltpu.SemaphoreType.DMA
    out = pl.pallas_call(
        kernel,
        out_shape=jax.ShapeDtypeStruct((tokens, WIDTH), BF16),
        in_specs=[pl.BlockSpec(memory_space=pltpu.SMEM)] + [anywhere] * 6,
        out_specs=vmem,
        scratch_shapes=[
            pltpu.VMEM((BLOCK, WIDTH), BF16),
            pltpu.VMEM((2, HEAD_DIM, WIDTH), BF16),
            pltpu.VMEM((4, 2 * BLOCK, WIDTH), BF16),
            pltpu.VMEM((4, 2, H3, WIDTH), BF16),
            pltpu.VMEM((HALF, H6, BLOCK), BF16),
            pltpu.VMEM((HALF, H6, BLOCK), BF16),
            pltpu.VMEM((HALF, H3, BLOCK), BF16),
            pltpu.VMEM((H3 + 16, N_CTX * BLOCK), BF16),
            pltpu.VMEM((H1, N_CTX * BLOCK), BF16),
            pltpu.VMEM((H2, N_CTX * BLOCK), F32),
            pltpu.VMEM((H2, HALF * BLOCK), F32),
            pltpu.VMEM((HALF, H1, BLOCK), BF16),
            pltpu.VMEM((HALF, H2, BLOCK), BF16),
            pltpu.VMEM((HALF, H1, BLOCK), BF16),
            pltpu.VMEM((HALF, H2, BLOCK), BF16),
            pltpu.VMEM((BLOCK, WIDTH), F32),
            pltpu.VMEM((BLOCK, WIDTH), BF16),
            dma((6,)),
            dma((3,)),
            dma((4,)),
            dma((3,)),
            dma((4,)),
            dma((HALF,)),
            dma((HALF,)),
            dma((HALF,)),
            dma((HALF,)),
            dma,
            dma,
            dma((HALF,)),
            dma((HALF,)),
            dma((HALF,)),
            dma((HALF,)),
            dma,
            dma,
        ],
        compiler_params=pltpu.CompilerParams(
            collective_id=0, has_side_effects=True, vmem_limit_bytes=48 * 2**20
        ),
    )(
        doc_ids,
        stay(activations[0, 0]),
        stay(out_grads[0, 0]),
        by_head(query_weight[0].T),
        by_head(key_weight[0].T),
        by_head(value_weight[0].T),
        by_head(out_weight[0]),
    )
    return out[None, None]


def solution(mesh):
    return jax.shard_map(
        body,
        mesh=mesh,
        in_specs=(
            P("section", "dp", "ctx", None),
            P("section", "dp", "ctx", None),
            P(),
            P("section", None, "dp"),
            P("section", None, "dp"),
            P("section", None, "dp"),
            P("section", "dp", None),
        ),
        out_specs=P("section", "dp", "ctx", None),
        check_vma=False,
    )
```

```python
import functools

import jax
import jax.numpy as jnp
from jax import lax
from jax.experimental import pallas as pl
from jax.experimental.pallas import tpu as pltpu
from jax.sharding import PartitionSpec as P

HEAD_DIM = 80
BLOCK = 128
WIDTH = 1280
N_CTX = 16
HALF = 8
SCALE = HEAD_DIM ** (-0.5)
NEG = -1e30
H1, H2, H3, H4, H6 = (n * HEAD_DIM for n in (1, 2, 3, 4, 6))
F32 = jnp.float32
BF16 = jnp.bfloat16
NT = (((1,), (1,)), ((), ()))


def dot(a, b):
    return jnp.dot(a, b, preferred_element_type=F32)


def dot_nt(a, b):
    return lax.dot_general(a, b, NT, preferred_element_type=F32)


def swap(two_bits):
    return 2 * (two_bits % 2) + two_bits // 2


def flip(matrix):
    return matrix.astype(F32).T.astype(BF16)


def split(wide):
    high = wide.astype(BF16)
    return high, (wide - high.astype(F32)).astype(BF16)


def kernel(
    docs_ref,
    x_hbm,
    og_hbm,
    wq_hbm,
    wk_hbm,
    wv_hbm,
    wg_hbm,
    out_ref,
    x_ref,
    wg_ref,
    acts,
    weights,
    send,
    recv,
    kv_other,
    keys3,
    values,
    kv_grad,
    kv_partial,
    back_q,
    back_kv,
    got_q,
    got_kv,
    total,
    branch_out,
    load_sem,
    act_send,
    act_recv,
    w_send,
    w_recv,
    send_sem,
    recv_sem,
    kv_send,
    kv_recv,
    part_send,
    part_recv,
    bq_send,
    bq_recv,
    bkv_send,
    bkv_recv,
    out_send,
    out_recv,
):
    section = lax.axis_index("section")
    n_section = lax.axis_size("section")
    z = lax.axis_index("ctx")
    dp = lax.axis_index("dp")
    x, c = dp // 2, dp % 2
    z_half, z_low, page = z // HALF, z % HALF, swap(z % 4)
    core_peer = {"dp": 2 * x + 1 - c}
    x_peer = {"dp": 2 * (1 - x) + c}
    before = {"section": (section + n_section - 1) % n_section}
    after = {"section": (section + 1) % n_section}
    alone = z_half == c
    alone_back = alone & (page == dp)
    late = page // 2 != x
    head = 4 * x + 2 * z_half + (z // 4) % 2

    def peer(index):
        return {"ctx": HALF * c + index, "dp": 2 * x + z_half}

    def peer_back(index):
        return {"ctx": HALF * c + index, "dp": page}

    def back_from(index):
        return {"ctx": HALF * ((index // 2) % 2) + 4 * (index % 2) + swap(dp), "dp": 2 * (index // 4) + z_half}

    barrier = pltpu.get_barrier_semaphore()
    for other in (core_peer, x_peer, after):
        pl.semaphore_signal(barrier, inc=1, device_id=other)

    def greet(index, carry):
        @pl.when(jnp.logical_not(alone & (index == z_low)))
        def _():
            pl.semaphore_signal(barrier, inc=1, device_id=peer(index))

        @pl.when(jnp.logical_not(alone_back & (index == head)))
        def _():
            pl.semaphore_signal(barrier, inc=1, device_id=back_from(index))

        return carry

    lax.fori_loop(0, HALF, greet, 0)

    loads = [
        pltpu.make_async_copy(source, target, load_sem.at[number])
        for number, (source, target) in enumerate(
            (
                (x_hbm, x_ref),
                (wq_hbm, weights.at[dp, :, pl.ds(0, H1)]),
                (wk_hbm, weights.at[dp, :, pl.ds(H1, H1)]),
                (wv_hbm, weights.at[dp, :, pl.ds(H2, H1)]),
                (og_hbm, acts.at[dp, pl.ds(BLOCK, BLOCK)]),
                (wg_hbm, wg_ref),
            )
        )
    ]
    for load in loads:
        load.start()

    rows = lax.broadcasted_iota(jnp.int32, (16, BLOCK), 0)
    for block in range(N_CTX):
        keys3[H3 : H3 + 16, block * BLOCK : (block + 1) * BLOCK] = jnp.where(
            (rows == docs_ref[page, block]) | (rows >= 4), 0.0, NEG
        ).astype(BF16)

    def page_of(r):
        return 2 * ((x + r // 2) % 2) + (c + r % 2) % 2

    def hand_on(buffer, r, target, send_ref, recv_ref):
        block = buffer.at[page_of(r)]
        return pltpu.make_async_remote_copy(
            src_ref=block, dst_ref=block, send_sem=send_ref, recv_sem=recv_ref, device_id=target
        )

    acts_to_x = hand_on(acts, 0, x_peer, act_send.at[0], act_recv.at[2])
    acts_to_core = hand_on(acts, 0, core_peer, act_send.at[1], act_recv.at[1])
    acts_relay = hand_on(acts, 2, core_peer, act_send.at[2], act_recv.at[3])
    weights_to_x = hand_on(weights, 0, x_peer, w_send.at[0], w_recv.at[2])
    weights_to_core = hand_on(weights, 0, core_peer, w_send.at[1], w_recv.at[1])
    weights_relay = hand_on(weights, 2, core_peer, w_send.at[2], w_recv.at[3])

    def here(buffer, r, recv_ref):
        block = buffer.at[page_of(r)]
        pltpu.make_async_copy(block, block, recv_ref.at[r]).wait()

    loads[0].wait()
    inputs = x_ref[...].astype(F32)
    inv_rms = lax.rsqrt(jnp.mean(inputs * inputs, axis=-1, keepdims=True) + 1e-05)
    acts[dp, 0:BLOCK] = (inputs * inv_rms).astype(BF16)
    for load in loads[1:]:
        load.wait()

    def send_copy(index):
        return pltpu.make_async_remote_copy(
            src_ref=send.at[index],
            dst_ref=recv.at[z_low],
            send_sem=send_sem.at[index],
            recv_sem=recv_sem.at[z_low],
            device_id=peer(index),
        )

    def project(slot, j):
        qkv = dot_nt(weights[dp, j], acts[slot, 0:BLOCK])
        out_grad = dot_nt(wg_ref[j], acts[slot, BLOCK : 2 * BLOCK])
        q_high, q_low = split(qkv[0:H1] * SCALE)
        k_high, k_low = split(qkv[H1:H2])
        unit = 4 * j + swap(slot)
        message = send.at[unit]
        message[0:H1] = q_high
        message[H1:H2] = q_low
        message[H2:H3] = out_grad.astype(BF16)
        message[H3:H4] = k_high
        message[H4 : H4 + H1] = k_low
        message[H4 + H1 : H6] = qkv[H2:H3].astype(BF16)

    def dispatch(unit):
        message = send.at[unit]
        mine = alone & (unit == z_low)

        @pl.when(mine)
        def _():
            pltpu.make_async_copy(message, recv.at[z_low], recv_sem.at[z_low]).start()

        @pl.when(jnp.logical_not(mine))
        def _():
            send_copy(unit).start()

    project(dp, 0)
    project(dp, 1)
    pl.semaphore_wait(barrier, 19 - alone.astype(jnp.int32) - alone_back.astype(jnp.int32))
    acts_to_x.start()
    acts_to_core.start()
    def step(turn, carry):
        r = 2 * (turn // 2) + (turn + c * (turn // 2)) % 2

        @pl.when(r == 1)
        def _():
            here(acts, 1, act_recv)

        @pl.when(turn == 2)
        def _():
            here(acts, 2, act_recv)
            acts_relay.start()
            weights_to_x.start()
            weights_to_core.start()

        @pl.when(r == 3)
        def _():
            here(acts, 3, act_recv)

        @pl.when(r > 0)
        def _():
            project(page_of(r), 0)
            project(page_of(r), 1)

        dispatch(swap(page_of(r)))
        dispatch(4 + swap(page_of(r)))
        return carry

    lax.fori_loop(0, 4, step, 0)

    def kv_copy(index):
        return pltpu.make_async_remote_copy(
            src_ref=recv.at[index, pl.ds(H3, H3)],
            dst_ref=kv_other.at[index],
            send_sem=kv_send.at[index],
            recv_sem=kv_recv.at[index],
            device_id=core_peer,
        )

    def place(block, kv):
        lanes = pl.ds(pl.multiple_of(block * BLOCK, BLOCK), BLOCK)
        keys3[0:H2, lanes] = kv[0:H2]
        keys3[H2:H3, lanes] = kv[0:H1]
        values[:, lanes] = kv[H2:H3]

    def arrive(index, carry):
        block = recv.at[index]
        pltpu.make_async_copy(block, block, recv_sem.at[index]).wait()
        kv_copy(index).start()
        place(HALF * c + index, recv[index, H3:H6])
        return carry

    lax.fori_loop(0, HALF, arrive, 0)

    def arrive_other(index, carry):
        kv_copy(index).wait_recv()
        place(HALF * (1 - c) + index, kv_other[index])
        return carry

    lax.fori_loop(0, HALF, arrive_other, 0)

    kv_grad[...] = jnp.zeros_like(kv_grad)

    def return_q(index):
        return pltpu.make_async_remote_copy(
            src_ref=back_q.at[index],
            dst_ref=got_q.at[head],
            send_sem=bq_send.at[index],
            recv_sem=bq_recv.at[head],
            device_id=peer_back(index),
        )

    def return_kv(index):
        return pltpu.make_async_remote_copy(
            src_ref=back_kv.at[index],
            dst_ref=got_kv.at[head],
            send_sem=bkv_send.at[index],
            recv_sem=bkv_recv.at[head],
            device_id=peer_back(index),
        )

    def give_q(index):
        mine = alone_back & (index == z_low)

        @pl.when(mine)
        def _():
            pltpu.make_async_copy(back_q.at[index], got_q.at[head], bq_recv.at[head]).start()

        @pl.when(jnp.logical_not(mine))
        def _():
            return_q(index).start()

    def in_order(step, count):
        return c * (count - 1) + (1 - 2 * c) * step

    def attend(step, carry):
        chunk = in_order(step, HALF // 2)
        one, two = recv.at[2 * chunk], recv.at[2 * chunk + 1]
        q_pair = jnp.concatenate([one[0:H2], two[0:H2]], axis=1)
        g_flat = jnp.concatenate([one[H2:H3], two[H2:H3]], axis=1)
        g = flip(g_flat)
        first = docs_ref[page, HALF * c + 2 * chunk]
        second = docs_ref[page, HALF * c + 2 * chunk + 1]
        shape = (16, 2 * BLOCK)
        lanes = lax.broadcasted_iota(jnp.int32, shape, 1)
        document = jnp.where(lanes < BLOCK, first, second)
        which = (lax.broadcasted_iota(jnp.int32, shape, 0) == document).astype(F32).astype(BF16)
        q3 = flip(jnp.concatenate([q_pair[0:H1], q_pair, which], axis=0))
        scores = dot(q3, keys3[...])
        top = jnp.max(scores, axis=-1, keepdims=True)
        weight = jnp.exp(scores - top)
        share = 1.0 / jnp.sum(weight, axis=-1, keepdims=True)
        prob = weight * share
        dprob = dot(g, values[...])
        delta = jnp.sum(prob * dprob, axis=-1, keepdims=True)
        dscore = (prob * (dprob - delta)).astype(BF16)
        q_grad = dot_nt(keys3[0:H2], dscore)
        q_grad = ((q_grad[0:H1] + q_grad[H1:H2]) * SCALE).astype(BF16)
        back_q[2 * chunk] = q_grad[:, 0:BLOCK]
        back_q[2 * chunk + 1] = q_grad[:, BLOCK:]
        k_grad = dot(q_pair, dscore)
        kv_grad[0:H1] += k_grad[0:H1] + k_grad[H1:H2]
        kv_grad[H1:H2] += dot(g_flat, prob.astype(BF16))
        if True:
            give_q(2 * chunk + c)
            give_q(2 * chunk + 1 - c)

        return carry

    lax.fori_loop(0, HALF // 2, attend, 0)

    def half_lanes(core):
        return pl.ds(pl.multiple_of(core * HALF * BLOCK, BLOCK), HALF * BLOCK)

    partial = pltpu.make_async_remote_copy(
        src_ref=kv_grad.at[:, half_lanes(1 - c)],
        dst_ref=kv_partial,
        send_sem=part_send,
        recv_sem=part_recv,
        device_id=core_peer,
    )
    partial.start()
    partial.wait_recv()

    def sent_all(index, carry):
        @pl.when(jnp.logical_not(alone & (index == z_low)))
        def _():
            send_copy(index).wait_send()

        return carry


    def finish_kv(step, carry):
        index = in_order(step, HALF)

        mine_lanes = pl.ds(pl.multiple_of((HALF * c + index) * BLOCK, BLOCK), BLOCK)
        lanes = pl.ds(pl.multiple_of(index * BLOCK, BLOCK), BLOCK)
        back_kv[index] = (kv_grad[:, mine_lanes] + kv_partial[:, lanes]).astype(BF16)
        mine = alone_back & (index == z_low)

        @pl.when(mine)
        def _():
            pltpu.make_async_copy(
                back_kv.at[index], got_kv.at[head], bkv_recv.at[head]
            ).start()

        @pl.when(jnp.logical_not(mine))
        def _():
            return_kv(index).start()

        return carry

    lax.fori_loop(0, HALF, finish_kv, 0)

    here(weights, 1, w_recv)
    here(weights, 2, w_recv)
    weights_relay.start()
    total[...] = jnp.zeros_like(total)
    here(weights, 3, w_recv)

    def combine(step, carry):
        index = (4 * x + step) % HALF
        q_block, kv_block = got_q.at[index], got_kv.at[index]
        pltpu.make_async_copy(q_block, q_block, bq_recv.at[index]).wait()
        pltpu.make_async_copy(kv_block, kv_block, bkv_recv.at[index]).wait()
        grads = jnp.concatenate([q_block[...], kv_block[...]], axis=0)
        total[...] += dot(flip(grads), weights[index // 2, index % 2])
        return carry

    lax.fori_loop(0, HALF, combine, 0)

    again = x_ref[...].astype(F32)
    rms = lax.rsqrt(jnp.mean(again * again, axis=-1, keepdims=True) + 1e-05)
    grad = total[...]
    branch_out[...] = (
        rms * grad - again * rms**3 * jnp.mean(grad * again, axis=-1, keepdims=True)
    ).astype(BF16)
    shift = pltpu.make_async_remote_copy(
        src_ref=branch_out,
        dst_ref=out_ref,
        send_sem=out_send,
        recv_sem=out_recv,
        device_id=before,
    )
    shift.start()

    for sent in (acts_to_x, acts_to_core, acts_relay):
        sent.wait_send()
    for sent in (weights_to_x, weights_to_core, weights_relay):
        sent.wait_send()
    partial.wait_send()

    def drain(index, carry):
        kv_copy(index).wait_send()

        @pl.when(jnp.logical_not(alone_back & (index == z_low)))
        def _():
            return_q(index).wait_send()
            return_kv(index).wait_send()

        return carry

    lax.fori_loop(0, HALF, drain, 0)
    lax.fori_loop(0, HALF, sent_all, 0)
    shift.wait()


def body(activations, out_grads, doc_ids, query_weight, key_weight, value_weight, out_weight):
    tokens = activations.shape[2]

    def stay(array):
        return pltpu.with_memory_space_constraint(array, pltpu.HBM)

    def by_head(rows):
        return stay(rows.reshape(2, HEAD_DIM, WIDTH))

    anywhere = pl.BlockSpec(memory_space=pl.ANY)
    vmem = pl.BlockSpec(memory_space=pltpu.VMEM)
    dma = pltpu.SemaphoreType.DMA
    out = pl.pallas_call(
        kernel,
        out_shape=jax.ShapeDtypeStruct((tokens, WIDTH), BF16),
        in_specs=[pl.BlockSpec(memory_space=pltpu.SMEM)] + [anywhere] * 6,
        out_specs=vmem,
        scratch_shapes=[
            pltpu.VMEM((BLOCK, WIDTH), BF16),
            pltpu.VMEM((2, HEAD_DIM, WIDTH), BF16),
            pltpu.VMEM((4, 2 * BLOCK, WIDTH), BF16),
            pltpu.VMEM((4, 2, H3, WIDTH), BF16),
            pltpu.VMEM((HALF, H6, BLOCK), BF16),
            pltpu.VMEM((HALF, H6, BLOCK), BF16),
            pltpu.VMEM((HALF, H3, BLOCK), BF16),
            pltpu.VMEM((H3 + 16, N_CTX * BLOCK), BF16),
            pltpu.VMEM((H1, N_CTX * BLOCK), BF16),
            pltpu.VMEM((H2, N_CTX * BLOCK), F32),
            pltpu.VMEM((H2, HALF * BLOCK), F32),
            pltpu.VMEM((HALF, H1, BLOCK), BF16),
            pltpu.VMEM((HALF, H2, BLOCK), BF16),
            pltpu.VMEM((HALF, H1, BLOCK), BF16),
            pltpu.VMEM((HALF, H2, BLOCK), BF16),
            pltpu.VMEM((BLOCK, WIDTH), F32),
            pltpu.VMEM((BLOCK, WIDTH), BF16),
            dma((6,)),
            dma((3,)),
            dma((4,)),
            dma((3,)),
            dma((4,)),
            dma((HALF,)),
            dma((HALF,)),
            dma((HALF,)),
            dma((HALF,)),
            dma,
            dma,
            dma((HALF,)),
            dma((HALF,)),
            dma((HALF,)),
            dma((HALF,)),
            dma,
            dma,
        ],
        compiler_params=pltpu.CompilerParams(
            collective_id=0, has_side_effects=True, vmem_limit_bytes=48 * 2**20
        ),
    )(
        doc_ids,
        stay(activations[0, 0]),
        stay(out_grads[0, 0]),
        by_head(query_weight[0].T),
        by_head(key_weight[0].T),
        by_head(value_weight[0].T),
        by_head(out_weight[0]),
    )
    return out[None, None]


def solution(mesh):
    return jax.shard_map(
        body,
        mesh=mesh,
        in_specs=(
            P("section", "dp", "ctx", None),
            P("section", "dp", "ctx", None),
            P(),
            P("section", None, "dp"),
            P("section", None, "dp"),
            P("section", None, "dp"),
            P("section", "dp", None),
        ),
        out_specs=P("section", "dp", "ctx", None),
        check_vma=False,
    )
```

```python
import functools

import jax
import jax.numpy as jnp
from jax import lax
from jax.experimental import pallas as pl
from jax.experimental.pallas import tpu as pltpu
from jax.sharding import PartitionSpec as P

HEAD_DIM = 80
BLOCK = 128
WIDTH = 1280
N_CTX = 16
HALF = 8
SCALE = HEAD_DIM ** (-0.5)
NEG = -1e30
H1, H2, H3, H4, H6 = (n * HEAD_DIM for n in (1, 2, 3, 4, 6))
F32 = jnp.float32
BF16 = jnp.bfloat16
NT = (((1,), (1,)), ((), ()))


def dot(a, b):
    return jnp.dot(a, b, preferred_element_type=F32)


def dot_nt(a, b):
    return lax.dot_general(a, b, NT, preferred_element_type=F32)


def swap(two_bits):
    return 2 * (two_bits % 2) + two_bits // 2


def flip(matrix):
    return matrix.astype(F32).T.astype(BF16)


def split(wide):
    high = wide.astype(BF16)
    return high, (wide - high.astype(F32)).astype(BF16)


def kernel(
    docs_ref,
    x_hbm,
    og_hbm,
    wq_hbm,
    wk_hbm,
    wv_hbm,
    wg_hbm,
    out_ref,
    x_ref,
    wg_ref,
    acts,
    weights,
    send,
    recv,
    kv_other,
    keys3,
    values,
    kv_grad,
    kv_partial,
    back_q,
    back_kv,
    got_q,
    got_kv,
    total,
    rms_kept,
    cubed,
    branch_out,
    load_sem,
    act_send,
    act_recv,
    w_send,
    w_recv,
    send_sem,
    recv_sem,
    kv_send,
    kv_recv,
    part_send,
    part_recv,
    bq_send,
    bq_recv,
    bkv_send,
    bkv_recv,
    out_send,
    out_recv,
):
    section = lax.axis_index("section")
    n_section = lax.axis_size("section")
    z = lax.axis_index("ctx")
    dp = lax.axis_index("dp")
    x, c = dp // 2, dp % 2
    z_half, z_low, page = z // HALF, z % HALF, swap(z % 4)
    core_peer = {"dp": 2 * x + 1 - c}
    x_peer = {"dp": 2 * (1 - x) + c}
    before = {"section": (section + n_section - 1) % n_section}
    after = {"section": (section + 1) % n_section}
    alone = z_half == c
    alone_back = alone & (page == dp)
    late = page // 2 != x
    head = 4 * x + 2 * z_half + (z // 4) % 2

    def peer(index):
        return {"ctx": HALF * c + index, "dp": 2 * x + z_half}

    def peer_back(index):
        return {"ctx": HALF * c + index, "dp": page}

    def back_from(index):
        return {"ctx": HALF * ((index // 2) % 2) + 4 * (index % 2) + swap(dp), "dp": 2 * (index // 4) + z_half}

    barrier = pltpu.get_barrier_semaphore()
    for other in (core_peer, x_peer, after):
        pl.semaphore_signal(barrier, inc=1, device_id=other)

    def greet(index, carry):
        @pl.when(jnp.logical_not(alone & (index == z_low)))
        def _():
            pl.semaphore_signal(barrier, inc=1, device_id=peer(index))

        @pl.when(jnp.logical_not(alone_back & (index == head)))
        def _():
            pl.semaphore_signal(barrier, inc=1, device_id=back_from(index))

        return carry

    lax.fori_loop(0, HALF, greet, 0)

    loads = [
        pltpu.make_async_copy(source, target, load_sem.at[number])
        for number, (source, target) in enumerate(
            (
                (x_hbm, x_ref),
                (wq_hbm, weights.at[dp, :, pl.ds(0, H1)]),
                (wk_hbm, weights.at[dp, :, pl.ds(H1, H1)]),
                (wv_hbm, weights.at[dp, :, pl.ds(H2, H1)]),
                (og_hbm, acts.at[dp, pl.ds(BLOCK, BLOCK)]),
                (wg_hbm, wg_ref),
            )
        )
    ]
    for load in loads:
        load.start()

    rows = lax.broadcasted_iota(jnp.int32, (16, BLOCK), 0)
    for block in range(N_CTX):
        keys3[H3 : H3 + 16, block * BLOCK : (block + 1) * BLOCK] = jnp.where(
            (rows == docs_ref[page, block]) | (rows >= 4), 0.0, NEG
        ).astype(BF16)

    def page_of(r):
        return 2 * ((x + r // 2) % 2) + (c + r % 2) % 2

    def hand_on(buffer, r, target, send_ref, recv_ref):
        block = buffer.at[page_of(r)]
        return pltpu.make_async_remote_copy(
            src_ref=block, dst_ref=block, send_sem=send_ref, recv_sem=recv_ref, device_id=target
        )

    acts_to_x = hand_on(acts, 0, x_peer, act_send.at[0], act_recv.at[2])
    acts_to_core = hand_on(acts, 0, core_peer, act_send.at[1], act_recv.at[1])
    acts_relay = hand_on(acts, 2, core_peer, act_send.at[2], act_recv.at[3])
    weights_to_x = hand_on(weights, 0, x_peer, w_send.at[0], w_recv.at[2])
    weights_to_core = hand_on(weights, 0, core_peer, w_send.at[1], w_recv.at[1])
    weights_relay = hand_on(weights, 2, core_peer, w_send.at[2], w_recv.at[3])

    def here(buffer, r, recv_ref):
        block = buffer.at[page_of(r)]
        pltpu.make_async_copy(block, block, recv_ref.at[r]).wait()

    loads[0].wait()
    inputs = x_ref[...].astype(F32)
    inv_rms = lax.rsqrt(jnp.mean(inputs * inputs, axis=-1, keepdims=True) + 1e-05)
    acts[dp, 0:BLOCK] = (inputs * inv_rms).astype(BF16)
    for load in loads[1:]:
        load.wait()

    def send_copy(index):
        return pltpu.make_async_remote_copy(
            src_ref=send.at[index],
            dst_ref=recv.at[z_low],
            send_sem=send_sem.at[index],
            recv_sem=recv_sem.at[z_low],
            device_id=peer(index),
        )

    def project(slot, j):
        qkv = dot_nt(weights[dp, j], acts[slot, 0:BLOCK])
        out_grad = dot_nt(wg_ref[j], acts[slot, BLOCK : 2 * BLOCK])
        q_high, q_low = split(qkv[0:H1] * SCALE)
        k_high, k_low = split(qkv[H1:H2])
        unit = 4 * j + swap(slot)
        message = send.at[unit]
        message[0:H1] = q_high
        message[H1:H2] = q_low
        message[H2:H3] = out_grad.astype(BF16)
        message[H3:H4] = k_high
        message[H4 : H4 + H1] = k_low
        message[H4 + H1 : H6] = qkv[H2:H3].astype(BF16)

    def dispatch(unit):
        message = send.at[unit]
        mine = alone & (unit == z_low)

        @pl.when(mine)
        def _():
            pltpu.make_async_copy(message, recv.at[z_low], recv_sem.at[z_low]).start()

        @pl.when(jnp.logical_not(mine))
        def _():
            send_copy(unit).start()

    project(dp, 0)
    project(dp, 1)
    pl.semaphore_wait(barrier, 19 - alone.astype(jnp.int32) - alone_back.astype(jnp.int32))
    acts_to_x.start()
    acts_to_core.start()
    def step(turn, carry):
        r = 2 * (turn // 2) + (turn + c * (turn // 2)) % 2

        @pl.when(r == 1)
        def _():
            here(acts, 1, act_recv)

        @pl.when(turn == 2)
        def _():
            here(acts, 2, act_recv)
            acts_relay.start()
            weights_to_x.start()
            weights_to_core.start()

        @pl.when(r == 3)
        def _():
            here(acts, 3, act_recv)

        for j in range(2):

            @pl.when(r > 0)
            def _():
                project(page_of(r), j)

            dispatch(4 * j + swap(page_of(r)))

        return carry

    lax.fori_loop(0, 4, step, 0)

    def kv_copy(index):
        return pltpu.make_async_remote_copy(
            src_ref=recv.at[index, pl.ds(H3, H3)],
            dst_ref=kv_other.at[index],
            send_sem=kv_send.at[index],
            recv_sem=kv_recv.at[index],
            device_id=core_peer,
        )

    def place(block, kv):
        lanes = pl.ds(pl.multiple_of(block * BLOCK, BLOCK), BLOCK)
        keys3[0:H2, lanes] = kv[0:H2]
        keys3[H2:H3, lanes] = kv[0:H1]
        values[:, lanes] = kv[H2:H3]

    def arrive(index, carry):
        block = recv.at[index]
        pltpu.make_async_copy(block, block, recv_sem.at[index]).wait()
        kv_copy(index).start()
        place(HALF * c + index, recv[index, H3:H6])
        return carry

    lax.fori_loop(0, HALF, arrive, 0)

    def arrive_other(index, carry):
        kv_copy(index).wait_recv()
        place(HALF * (1 - c) + index, kv_other[index])
        return carry

    lax.fori_loop(0, HALF, arrive_other, 0)

    kv_grad[...] = jnp.zeros_like(kv_grad)

    def return_q(index):
        return pltpu.make_async_remote_copy(
            src_ref=back_q.at[index],
            dst_ref=got_q.at[head],
            send_sem=bq_send.at[index],
            recv_sem=bq_recv.at[head],
            device_id=peer_back(index),
        )

    def return_kv(index):
        return pltpu.make_async_remote_copy(
            src_ref=back_kv.at[index],
            dst_ref=got_kv.at[head],
            send_sem=bkv_send.at[index],
            recv_sem=bkv_recv.at[head],
            device_id=peer_back(index),
        )

    def give_q(index):
        mine = alone_back & (index == z_low)

        @pl.when(mine)
        def _():
            pltpu.make_async_copy(back_q.at[index], got_q.at[head], bq_recv.at[head]).start()

        @pl.when(jnp.logical_not(mine))
        def _():
            return_q(index).start()

    def in_order(step, count):
        return c * (count - 1) + (1 - 2 * c) * step

    def attend(step, carry):
        chunk = in_order(step, HALF // 2)
        one, two = recv.at[2 * chunk], recv.at[2 * chunk + 1]
        q_pair = jnp.concatenate([one[0:H2], two[0:H2]], axis=1)
        g_flat = jnp.concatenate([one[H2:H3], two[H2:H3]], axis=1)
        g = flip(g_flat)
        first = docs_ref[page, HALF * c + 2 * chunk]
        second = docs_ref[page, HALF * c + 2 * chunk + 1]
        shape = (16, 2 * BLOCK)
        lanes = lax.broadcasted_iota(jnp.int32, shape, 1)
        document = jnp.where(lanes < BLOCK, first, second)
        which = (lax.broadcasted_iota(jnp.int32, shape, 0) == document).astype(F32).astype(BF16)
        q3 = flip(jnp.concatenate([q_pair[0:H1], q_pair, which], axis=0))
        scores = dot(q3, keys3[...])
        top = jnp.max(scores, axis=-1, keepdims=True)
        weight = jnp.exp(scores - top)
        share = 1.0 / jnp.sum(weight, axis=-1, keepdims=True)
        prob = weight * share
        dprob = dot(g, values[...])
        delta = jnp.sum(prob * dprob, axis=-1, keepdims=True)
        dscore = (prob * (dprob - delta)).astype(BF16)
        q_grad = dot_nt(keys3[0:H2], dscore)
        q_grad = ((q_grad[0:H1] + q_grad[H1:H2]) * SCALE).astype(BF16)
        back_q[2 * chunk] = q_grad[:, 0:BLOCK]
        back_q[2 * chunk + 1] = q_grad[:, BLOCK:]
        k_grad = dot(q_pair, dscore)
        kv_grad[0:H1] += k_grad[0:H1] + k_grad[H1:H2]
        kv_grad[H1:H2] += dot(g_flat, prob.astype(BF16))
        if True:
            give_q(2 * chunk + c)
            give_q(2 * chunk + 1 - c)

        return carry

    lax.fori_loop(0, HALF // 2, attend, 0)

    def half_lanes(core):
        return pl.ds(pl.multiple_of(core * HALF * BLOCK, BLOCK), HALF * BLOCK)

    partial = pltpu.make_async_remote_copy(
        src_ref=kv_grad.at[:, half_lanes(1 - c)],
        dst_ref=kv_partial,
        send_sem=part_send,
        recv_sem=part_recv,
        device_id=core_peer,
    )
    partial.start()
    partial.wait_recv()

    def sent_all(index, carry):
        @pl.when(jnp.logical_not(alone & (index == z_low)))
        def _():
            send_copy(index).wait_send()

        return carry


    def finish_kv(step, carry):
        index = in_order(step, HALF)

        mine_lanes = pl.ds(pl.multiple_of((HALF * c + index) * BLOCK, BLOCK), BLOCK)
        lanes = pl.ds(pl.multiple_of(index * BLOCK, BLOCK), BLOCK)
        back_kv[index] = (kv_grad[:, mine_lanes] + kv_partial[:, lanes]).astype(BF16)
        mine = alone_back & (index == z_low)

        @pl.when(mine)
        def _():
            pltpu.make_async_copy(
                back_kv.at[index], got_kv.at[head], bkv_recv.at[head]
            ).start()

        @pl.when(jnp.logical_not(mine))
        def _():
            return_kv(index).start()

        return carry

    lax.fori_loop(0, HALF, finish_kv, 0)

    here(weights, 1, w_recv)
    here(weights, 2, w_recv)
    weights_relay.start()
    again = x_ref[...].astype(F32)
    rms = lax.rsqrt(jnp.mean(again * again, axis=-1, keepdims=True) + 1e-05)
    rms_kept[...] = rms
    cubed[...] = again * rms**3
    total[...] = jnp.zeros_like(total)
    here(weights, 3, w_recv)

    def combine(step, carry):
        index = (4 * x + step) % HALF
        q_block, kv_block = got_q.at[index], got_kv.at[index]
        pltpu.make_async_copy(q_block, q_block, bq_recv.at[index]).wait()
        pltpu.make_async_copy(kv_block, kv_block, bkv_recv.at[index]).wait()
        grads = jnp.concatenate([q_block[...], kv_block[...]], axis=0)
        total[...] += dot(flip(grads), weights[index // 2, index % 2])
        return carry

    lax.fori_loop(0, HALF, combine, 0)

    grad = total[...]
    lean = jnp.mean(grad * x_ref[...].astype(F32), axis=-1, keepdims=True)
    branch_out[...] = (rms_kept[...] * grad - cubed[...] * lean).astype(BF16)
    shift = pltpu.make_async_remote_copy(
        src_ref=branch_out,
        dst_ref=out_ref,
        send_sem=out_send,
        recv_sem=out_recv,
        device_id=before,
    )
    shift.start()

    for sent in (acts_to_x, acts_to_core, acts_relay):
        sent.wait_send()
    for sent in (weights_to_x, weights_to_core, weights_relay):
        sent.wait_send()
    partial.wait_send()

    def drain(index, carry):
        kv_copy(index).wait_send()

        @pl.when(jnp.logical_not(alone_back & (index == z_low)))
        def _():
            return_q(index).wait_send()
            return_kv(index).wait_send()

        return carry

    lax.fori_loop(0, HALF, drain, 0)
    lax.fori_loop(0, HALF, sent_all, 0)
    shift.wait()


def body(activations, out_grads, doc_ids, query_weight, key_weight, value_weight, out_weight):
    tokens = activations.shape[2]

    def stay(array):
        return pltpu.with_memory_space_constraint(array, pltpu.HBM)

    def by_head(rows):
        return stay(rows.reshape(2, HEAD_DIM, WIDTH))

    anywhere = pl.BlockSpec(memory_space=pl.ANY)
    vmem = pl.BlockSpec(memory_space=pltpu.VMEM)
    dma = pltpu.SemaphoreType.DMA
    out = pl.pallas_call(
        kernel,
        out_shape=jax.ShapeDtypeStruct((tokens, WIDTH), BF16),
        in_specs=[pl.BlockSpec(memory_space=pltpu.SMEM)] + [anywhere] * 6,
        out_specs=vmem,
        scratch_shapes=[
            pltpu.VMEM((BLOCK, WIDTH), BF16),
            pltpu.VMEM((2, HEAD_DIM, WIDTH), BF16),
            pltpu.VMEM((4, 2 * BLOCK, WIDTH), BF16),
            pltpu.VMEM((4, 2, H3, WIDTH), BF16),
            pltpu.VMEM((HALF, H6, BLOCK), BF16),
            pltpu.VMEM((HALF, H6, BLOCK), BF16),
            pltpu.VMEM((HALF, H3, BLOCK), BF16),
            pltpu.VMEM((H3 + 16, N_CTX * BLOCK), BF16),
            pltpu.VMEM((H1, N_CTX * BLOCK), BF16),
            pltpu.VMEM((H2, N_CTX * BLOCK), F32),
            pltpu.VMEM((H2, HALF * BLOCK), F32),
            pltpu.VMEM((HALF, H1, BLOCK), BF16),
            pltpu.VMEM((HALF, H2, BLOCK), BF16),
            pltpu.VMEM((HALF, H1, BLOCK), BF16),
            pltpu.VMEM((HALF, H2, BLOCK), BF16),
            pltpu.VMEM((BLOCK, WIDTH), F32),
            pltpu.VMEM((BLOCK, 1), F32),
            pltpu.VMEM((BLOCK, WIDTH), F32),
            pltpu.VMEM((BLOCK, WIDTH), BF16),
            dma((6,)),
            dma((3,)),
            dma((4,)),
            dma((3,)),
            dma((4,)),
            dma((HALF,)),
            dma((HALF,)),
            dma((HALF,)),
            dma((HALF,)),
            dma,
            dma,
            dma((HALF,)),
            dma((HALF,)),
            dma((HALF,)),
            dma((HALF,)),
            dma,
            dma,
        ],
        compiler_params=pltpu.CompilerParams(
            collective_id=0, has_side_effects=True, vmem_limit_bytes=48 * 2**20
        ),
    )(
        doc_ids,
        stay(activations[0, 0]),
        stay(out_grads[0, 0]),
        by_head(query_weight[0].T),
        by_head(key_weight[0].T),
        by_head(value_weight[0].T),
        by_head(out_weight[0]),
    )
    return out[None, None]


def solution(mesh):
    return jax.shard_map(
        body,
        mesh=mesh,
        in_specs=(
            P("section", "dp", "ctx", None),
            P("section", "dp", "ctx", None),
            P(),
            P("section", None, "dp"),
            P("section", None, "dp"),
            P("section", None, "dp"),
            P("section", "dp", None),
        ),
        out_specs=P("section", "dp", "ctx", None),
        check_vma=False,
    )
```
